32 devices in a mesh: bins: 16 (over z, y, x), diag: 2 (over core).
Axes of the slice: x: 2, y: 2, z: 4, core: 2. Of those that a mesh axis runs over, the one named last changes fastest.
Arguments:
- held_tiles: float32 [32, 2, 1024, 1024], P('bins', 'diag'), may hold values from 0.01 to 20, as said below
- placed: int32 [32], P('bins'), may hold values from 0 to 1, as said below
- bin_mask: int32 [32768], P('bins'), may hold values 0 or 1
- bias: float32 [32768], P('bins'), may hold values from 0.5 to 2
Outputs:
- balanced: float32 [32, 2, 1024, 1024], P('bins', 'diag')
- bias_out: float32 [32768], P('bins')
The draws below stay inside these ranges and needn't reach their ends.
Inputs may be any that keep to these rules, and one draw needn't show every extreme that they name: placed[q] equals placed[(q + 16) mod 32]; placed[q] is 1 where q is a multiple of 2. `held_tiles`: entries are positive.
All inputs are finite; a program needn't handle non-finite values. No bound on the sum of `bin_mask` on one device may be relied on, other than what follows from the above.
Results may differ from the reference program's by a relative error of at most 0.00012.
Values sent between devices are 32-bit elements; how exact they have to be, the bound alone decides.
A program may use at most 128 MiB of HBM per device.

```python
import math
import jax
import jax.numpy as jnp

TILE = 1024
TILES_DEV = 2
ITERS = 2
TILE_ROWS = 32
BINS = 32768


def draw_placed(key, part):
    half_flags = jax.random.randint(jax.random.fold_in(key, 11), (TILE_ROWS // 2,), 0, 2).astype(jnp.int32)
    first_rows = jnp.arange(TILE_ROWS // 2, dtype=jnp.int32) % TILES_DEV == 0
    half_flags = jnp.where(first_rows, 1, half_flags).astype(jnp.int32)
    return jnp.concatenate([half_flags, half_flags])


def draw_held_tiles(key, part):
    lines = jnp.arange(TILE, dtype=jnp.float32)
    offsets = jnp.arange(2, dtype=jnp.float32)
    distance = jnp.abs(offsets[:, None, None] * TILE + lines[None, None, :] - lines[None, :, None])
    decay = 1.0 / (1.0 + distance / 256.0)
    position = jnp.arange(TILE_ROWS, dtype=jnp.float32) / max(TILE_ROWS - 1, 1)
    shape = (TILE_ROWS, 2, TILE, TILE)
    noise = jnp.exp(jax.random.uniform(jax.random.fold_in(key, 22), shape, jnp.float32, -1.0, 1.0))
    rise = 1.0 + 2.0 * position
    return (noise * decay[None] * rise[:, None, None, None]).astype(jnp.float32)


def plant(drawn, stream_key, smallest, high):
    index_at = [jax.random.randint(jax.random.fold_in(stream_key, axis), (), 0, length) for axis, length in enumerate(drawn.shape)]
    longest = drawn.shape.index(max(drawn.shape))
    neighbour = index_at[:longest] + [(index_at[longest] + 1) % drawn.shape[longest]] + index_at[longest + 1:]
    return drawn.at[tuple(index_at)].set(smallest).at[tuple(neighbour)].set(high)


def block_scale(rng, extent, cuts, least, high):
    factor_of, own = 1.0, jax.random.fold_in(rng, 6)
    for axis_at, blocks in cuts:
        heights = jnp.exp(jax.random.uniform(jax.random.fold_in(own, axis_at), (blocks,), jnp.float32, least / len(cuts), high / len(cuts)))
        factor_of = factor_of * jnp.repeat(heights, extent[axis_at] // blocks).reshape([-1 if axis == axis_at else 1 for axis in range(len(extent))])
    return factor_of


def setup_inputs(seed: int = 0) -> dict:
    seeds = jax.random.split(jax.random.key(seed), 5)
    return {
        "held_tiles": draw_held_tiles(jax.random.fold_in(seeds[4], 71), 0),
        "placed": draw_placed(jax.random.fold_in(seeds[4], 71), 0),
        "bin_mask": plant((jax.random.randint(seeds[2], (BINS,), 0, 10) < 9).astype(jnp.int32), jax.random.fold_in(seeds[2], 1), 0, 1),
        "bias": jnp.clip(jnp.exp(math.log(2.0) - 1.3862944 * jax.random.uniform(seeds[3], (BINS,), jnp.float32) ** block_scale(seeds[3], (BINS,), ((0, 16),), -0.2, 0.2)), 0.5, 2.0),
    }


def reference(held_tiles, placed, bin_mask, bias):
    row_index = jnp.arange(TILE_ROWS, dtype=jnp.int32)
    partner = (row_index + TILE_ROWS // 2) % TILE_ROWS
    source = jnp.where(placed == 1, partner, row_index).astype(jnp.int32)
    home_tiles = held_tiles[source]
    live = bin_mask.astype(jnp.float32).reshape(TILE_ROWS, TILE)
    empty_row = jnp.zeros((1, TILE), jnp.float32)
    live_next = jnp.concatenate([live[1:], empty_row], axis=0)
    lines = jnp.arange(TILE, dtype=jnp.int32)
    upper_mask = (lines[:, None] <= lines[None, :]).astype(jnp.float32)
    diag_block = home_tiles[:, 0] * upper_mask * live[:, :, None] * live[:, None, :]
    off_block = home_tiles[:, 1] * live[:, :, None] * live_next[:, None, :]
    bias_now = bias.reshape(TILE_ROWS, TILE)
    for repeat in range(ITERS):
        row_diag = jnp.sum(diag_block, axis=2)
        col_diag = jnp.sum(diag_block, axis=1) - jnp.diagonal(diag_block, axis1=1, axis2=2)
        row_off = jnp.sum(off_block, axis=2)
        col_off = jnp.sum(off_block, axis=1)
        sums = row_diag + col_diag + row_off + jnp.concatenate([empty_row, col_off[:-1]], axis=0)
        masked_total = jnp.sum(sums * live)
        live_count = jnp.sum(live)
        mean_sum = masked_total / live_count
        factor = jnp.where(live > 0, sums / mean_sum, 1.0)
        bias_now = bias_now * factor
        inverse = 1.0 / factor
        inverse_next = jnp.concatenate([inverse[1:], empty_row], axis=0)
        diag_block = diag_block * inverse[:, :, None] * inverse[:, None, :]
        off_block = off_block * inverse[:, :, None] * inverse_next[:, None, :]
    balanced = jnp.stack([diag_block, off_block], axis=1)
    return balanced, bias_now.reshape(BINS)
```

```python
import functools

import jax
import jax.numpy as jnp
from jax import lax
from jax.experimental import pallas as pl
from jax.experimental.pallas import tpu as pltpu
from jax.sharding import PartitionSpec as P

ITERS = 2
B = 128
SUBS = 8
MESH = pl.DeviceIdType.MESH
F32 = jnp.float32


def first(n, size, held, placed, mask, bias, arr0, pieces, flags_out, u_out, v_out, bias_out, diag_out,
          home, pack, p_mask, next_mask, live2, live_col2, nlive2, stored_row, stored_col, u2, v2, su, sv, row, col_acc, diag_vec, raw_vec, raw_in,
          quad, edge_out, edge_in, edge_pair, nxt, tot, sums_now,
          in_sem, mask_sem, nmask_sem, bulk_sem, scat_sem, own_sem, raw_sem, quad_sem, edge_sem, epair_sem, nxt_sem, tot_sem):
    b, d = lax.axis_index("bins"), lax.axis_index("diag")
    half = n // 2
    count = n * 2
    me = b * 2 + d
    on_diag, off_diag = d == 0, d == 1
    strips = size // B
    group = strips
    width = 2 * size
    part = B // 2
    side = b // half
    spot_l = lax.rem(b, half)
    partner = (lax.rem(b + half, n), d)
    slot = side * 2 + d
    prev_l, next_l = lax.rem(spot_l + half - 1, half), lax.rem(spot_l + 1, half)
    place_in = lax.rem(b, group)
    base_chip = b - place_in

    def remote(src, dst, send, recv, device):
        return pltpu.make_async_remote_copy(src, dst, send, recv, device_id=device, device_id_type=MESH)

    def other(off):
        target = lax.rem(me + off, count)
        return (target // 2, lax.rem(target, 2))

    barrier = pltpu.get_barrier_semaphore()

    def greet(off, carry):
        pl.semaphore_signal(barrier, inc=1, device_id=other(off), device_id_type=MESH)
        return carry

    lax.fori_loop(1, count, greet, 0)
    loads = []
    for t in range(2):
        loads.append(pltpu.make_async_copy(held.at[t, 0], home.at[t], in_sem.at[t]))
        loads[-1].start()
    pl.semaphore_wait(barrier, count - 1)

    mask_send = remote(mask, p_mask, mask_sem.at[0], mask_sem.at[1], partner)
    mask_send.start()
    nmask = [remote(mask.at[:, :size], next_mask.at[side], nmask_sem.at[i], nmask_sem.at[2 + side], (prev_l + i * half, 1)) for i in range(2)]

    @pl.when(on_diag)
    def _():
        for copy in nmask:
            copy.start()

    def rows_of(e, tall):
        return pl.ds(pl.multiple_of(e * tall, tall), tall)

    def bulk(e):
        diag_part = remote(pack.at[0, e // 2, pl.ds((e % 2) * part, part)], arr0.at[e, :part], bulk_sem.at[0], bulk_sem.at[1], partner)
        off_part = remote(held.at[0, 0, pl.ds(e * B, B)], arr0.at[e], bulk_sem.at[0], bulk_sem.at[1], partner)
        return diag_part, off_part

    def start_bulk(pieces_now):
        @pl.when(on_diag)
        def _():
            for e in pieces_now:
                bulk(e)[0].start()

        @pl.when(off_diag)
        def _():
            for e in pieces_now:
                bulk(e)[1].start()

    def start_scatter(off, carry):
        e = lax.rem(place_in + off, group)

        @pl.when(on_diag)
        def _():
            remote(pack.at[1, e // 2, rows_of(lax.rem(e, 2), part)], pieces.at[place_in, :part], scat_sem.at[0], scat_sem.at[1], (base_chip + e, d)).start()

        @pl.when(off_diag)
        def _():
            remote(held.at[1, 0, rows_of(e, B)], pieces.at[place_in], scat_sem.at[0], scat_sem.at[1], (base_chip + e, d)).start()

        return carry

    line = lax.broadcasted_iota(jnp.int32, (B, B), 0)
    lane = lax.broadcasted_iota(jnp.int32, (B, B), 1)

    def fold_tile(t):
        for j in range(strips // 2):
            k = strips - 1 - j
            low, high = home[t, j * B:(j + 1) * B, j * B:(j + 1) * B], home[t, k * B:(k + 1) * B, k * B:(k + 1) * B]
            pack[t, j, :, :B] = jnp.where(line <= lane, low, high.T)
            mid = (strips - j) * B
            pack[t, j, :, B:mid] = home[t, j * B:(j + 1) * B, (j + 1) * B:]
            if mid < size:
                pack[t, j, :, mid:] = home[t, k * B:(k + 1) * B, (k + 1) * B:]

            for q, block in ((j, low), (k, high)):
                raw_vec[:, t * size + q * B:t * size + (q + 1) * B] = jnp.sum(jnp.where(line == lane, block, 0.0), axis=0, keepdims=True)

    own_off = pltpu.make_async_copy(home.at[1, rows_of(place_in, B)], pieces.at[place_in], own_sem.at[0])
    own_diag = pltpu.make_async_copy(pack.at[1, place_in // 2, rows_of(lax.rem(place_in, 2), part)], pieces.at[place_in, :part], own_sem.at[0])
    raw_send = remote(raw_vec, raw_in, raw_sem.at[0], raw_sem.at[1], partner)

    early, middle, late = range(0, strips // 4), range(strips // 4, strips // 2), range(strips // 2, strips)

    @pl.when(off_diag)
    def _():
        for e in early:
            bulk(e)[1].start()

    for t in range(2):
        loads[t].wait()

    @pl.when(on_diag)
    def _():
        fold_tile(0)
        for e in early:
            bulk(e)[0].start()
        fold_tile(1)
        own_diag.start()
        raw_send.start()

    @pl.when(off_diag)
    def _():
        own_off.start()

    mask_send.wait()

    @pl.when(off_diag)
    def _():
        for i in range(2):
            remote(mask.at[:, :size], next_mask.at[i], nmask_sem.at[0], nmask_sem.at[2 + i], partner).wait_recv()

    @pl.when(on_diag)
    def _():
        for copy in nmask:
            copy.wait_send()

    def pair_of(own, their):
        lower, upper = jnp.where(side == 0, own, their), jnp.where(side == 0, their, own)
        return jnp.concatenate([lower, upper], axis=0)

    def own_of(both):
        return jnp.where(side == 0, both[0:1], both[1:2])

    flag = jnp.full((1, size), placed[1]) == 1
    gone = jnp.concatenate([jnp.ones((1, size), jnp.int32), flag.astype(jnp.int32)], axis=1)
    at_side = jnp.where(gone == 1, 1 - side, side)

    def stored(both):
        return jnp.where(at_side == 0, both[0:1], both[1:2])

    sides = lax.broadcasted_iota(jnp.int32, (2, width), 0)

    def put_home(vector):
        return jnp.where(sides == at_side, vector, 0.0)

    def from_next(both):
        return jnp.where(spot_l == half - 1, jnp.concatenate([both[1:2], jnp.zeros_like(both[0:1])], axis=0), both)

    def from_prev(both):
        return jnp.where(spot_l == 0, jnp.concatenate([jnp.zeros_like(both[0:1]), both[0:1]], axis=0), both)

    live2[...] = pair_of(mask[...].astype(F32), p_mask[...].astype(F32))
    nlive2[...] = jnp.zeros_like(nlive2)

    @pl.when(off_diag)
    def _():
        nlive2[...] = from_next(jnp.concatenate([next_mask[0], next_mask[1]], axis=0).astype(F32))

    live_col2[...] = jnp.where(on_diag, live2[...], jnp.concatenate([live2[:, size:], nlive2[...]], axis=1))
    stored_row[...] = stored(live2[...])
    stored_col[...] = stored(live_col2[...])
    u2[...] = jnp.ones_like(u2)
    v2[...] = jnp.ones_like(v2)
    su[...] = jnp.ones_like(su)
    sv[...] = jnp.ones_like(sv)
    bias_out[...] = bias[...]
    shift = jnp.where(on_diag, 0, -2 * size)

    def down(vector):
        return jnp.broadcast_to(vector, (B, B)).T

    def folded(block):
        return jnp.sum(block.reshape(B // 8, 8, B), axis=0)

    first_lane = lax.broadcasted_iota(jnp.int32, (1, B), 1)

    def settle(k):
        many = tot.at[k, pl.ds(0, count - 1)]
        pltpu.make_async_copy(many, many, tot_sem.at[k, 0]).wait()
        pltpu.make_async_copy(many, many, tot_sem.at[k, 1]).wait()
        both = jnp.sum(tot[k], axis=0)
        mean = jnp.sum(jnp.where(first_lane == 0, both, 0.0), axis=1, keepdims=True) / jnp.sum(
            jnp.where(first_lane == 1, both, 0.0), axis=1, keepdims=True)
        bias_out[...] = bias_out[...] * jnp.where(mask[...] > 0, sums_now[...] / mean, 1.0)
        u2[...] = u2[...] * jnp.where(live2[...] > 0, mean, 1.0)
        v2[...] = v2[...] * jnp.where(live_col2[...] > 0, mean, 1.0)
        return mean

    for k in range(ITERS):
        col_acc[...] = jnp.zeros_like(col_acc)
        for t in range(2):
            if k == 0 and t == 1:
                @pl.when(off_diag)
                def _():
                    own_off.wait()

            def strip_pass(r, carry):
                rows = rows_of(r, B)
                spot = pl.ds(pl.multiple_of(t * size + r * B, B), B)
                total = jnp.zeros((B, B), F32)
                if k == 0:
                    live_down = down(stored_row[:, spot])
                    for c in range(strips):
                        block = home[t, rows, c * B:(c + 1) * B]
                        keep = line + (r * B + shift) <= lane + c * B
                        block = jnp.where(keep, block, 0.0) * live_down * stored_col[:, t * size + c * B:t * size + (c + 1) * B]
                        home[t, rows, c * B:(c + 1) * B] = block
                        col_acc[t, :, c * B:(c + 1) * B] += folded(block)
                        total = total + block
                    corner = home[t, rows, rows]
                    diag_vec[:, spot] = jnp.where(on_diag, jnp.sum(jnp.where(line == lane, corner, 0.0), axis=0, keepdims=True), 0.0)
                else:
                    u_down = down(su[:, spot])
                    for c in range(strips):
                        block = home[t, rows, c * B:(c + 1) * B]
                        col_acc[t, :, c * B:(c + 1) * B] += folded(block * u_down)
                        total = total + block * sv[:, t * size + c * B:t * size + (c + 1) * B]
                row[:, spot] = jnp.sum(total.T, axis=0, keepdims=True)
                return carry

            lax.fori_loop(0, strips, strip_pass, 0)

        cols = jnp.concatenate([jnp.sum(col_acc[t], axis=0, keepdims=True) for t in range(2)], axis=1) * sv[...]
        rows2 = put_home(row[...] * su[...])
        corner2 = put_home(diag_vec[...] * su[...] * sv[...])
        cols2 = put_home(cols)
        zero = jnp.zeros((2, size), F32)
        mine = rows2 + jnp.where(on_diag, cols2 - corner2, jnp.concatenate([zero, cols2[:, :size]], axis=1))
        edge = jnp.where(on_diag, 0.0, cols2[:, size:])
        if k > 0:
            mean = settle(k - 1)
            mine, edge = (jnp.where(value != 0, value * mean * mean, 0.0) for value in (mine, edge))
        quad[k, slot] = mine
        edge_out[k] = edge
        partial = jnp.sum(mine) + jnp.sum(edge)
        kept = jnp.where(on_diag, jnp.sum(mask[...].astype(F32)), 0.0)
        marked = jnp.full((1, B), placed[1]).astype(F32)
        tot[k, me] = jnp.where(first_lane == 0, partial, jnp.where(first_lane == 1, kept, jnp.where(first_lane == 2, marked, 0.0)))

        def quad_copy(off):
            q = lax.rem(slot + off, 4)
            return remote(quad.at[k, slot], quad.at[k, slot], quad_sem.at[k, 0], quad_sem.at[k, 1], (spot_l + (q // 2) * half, lax.rem(q, 2)))

        nxt_copies = [remote(quad.at[k, slot, :, :size], nxt.at[k, slot], nxt_sem.at[k, 0], nxt_sem.at[k, 1], (prev_l + i * half, 1)) for i in range(2)]
        edge_copies = [remote(edge_out.at[k], edge_in.at[k, side], edge_sem.at[k, 0], edge_sem.at[k, 1], (next_l + (i // 2) * half, i % 2)) for i in range(4)]
        epair = remote(edge_out.at[k], edge_pair.at[k], epair_sem.at[k, 0], epair_sem.at[k, 1], partner)

        for off in range(1, 4):
            quad_copy(off).start()
        for copy in nxt_copies:
            copy.start()

        @pl.when(off_diag)
        def _():
            for copy in edge_copies:
                copy.start()
            epair.start()

        def tot_start(off, carry):
            remote(tot.at[k, me], tot.at[k, me], tot_sem.at[k, 0], tot_sem.at[k, 1], other(off)).start()
            return carry

        lax.fori_loop(1, count, tot_start, 0)

        if k < ITERS - 1:
            start_bulk(middle)
        else:
            lax.fori_loop(1, group, start_scatter, 0)
            start_bulk(late)

        def wait_all(ref, sem):
            pltpu.make_async_copy(ref, ref, sem).wait()

        wait_all(quad.at[k, pl.ds(0, 3)], quad_sem.at[k, 1])
        wait_all(edge_in.at[k], edge_sem.at[k, 1])

        @pl.when(off_diag)
        def _():
            wait_all(nxt.at[k], nxt_sem.at[k, 1])
            epair.wait_recv()

        wait_all(quad.at[k, pl.ds(0, 3)], quad_sem.at[k, 0])
        wait_all(nxt.at[k, pl.ds(0, 2)], nxt_sem.at[k, 0])

        @pl.when(off_diag)
        def _():
            wait_all(edge_in.at[k], edge_sem.at[k, 0])
            wait_all(edge_in.at[k], edge_sem.at[k, 0])
            epair.wait_send()

        sums = (quad[k, 0] + quad[k, 1]) + (quad[k, 2] + quad[k, 3])
        arrived = from_prev(edge_in[k, 0] + edge_in[k, 1])
        sums = sums + jnp.concatenate([arrived, jnp.zeros((2, size), F32)], axis=1)
        sums_now[...] = own_of(sums)
        inverse = 1.0 / jnp.where(live2[...] > 0, sums, 1.0)
        u2[...] = u2[...] * inverse

        @pl.when(on_diag)
        def _():
            v2[...] = v2[...] * inverse

        @pl.when(off_diag)
        def _():
            next_sums = from_next((nxt[k, 0] + nxt[k, 1]) + (nxt[k, 2] + nxt[k, 3])) + (edge_out[k] + edge_pair[k])
            next_inverse = 1.0 / jnp.where(nlive2[...] > 0, next_sums, 1.0)
            v2[...] = v2[...] * jnp.concatenate([inverse[:, size:], next_inverse], axis=1)

        su[...] = stored(u2[...])
        sv[...] = stored(v2[...])

    settle(ITERS - 1)
    u_out[...] = own_of(jnp.where(live2[...] > 0, u2[...], 0.0))
    v_out[...] = own_of(jnp.where(live_col2[...] > 0, v2[...], 0.0))

    best = None
    for g in range(half // group):
        several = tot[0, g * group * 2]
        for p in range(1, group):
            several = several + tot[0, (g * group + p) * 2]
        best = several if best is None else jnp.maximum(best, several)
    flags_out[group] = jnp.sum(jnp.where(first_lane == 2, best, 0.0)).astype(jnp.int32)
    for p in range(group):
        flags_out[p] = jnp.sum(jnp.where(first_lane == 2, tot[0, (base_chip + p) * 2], 0.0)).astype(jnp.int32)

    diag_out[...] = jnp.zeros_like(diag_out)

    @pl.when(on_diag)
    def _():
        raw_send.wait()
        diag_out[...] = jnp.where(gone == 1, raw_in[...], raw_vec[...])
        own_diag.wait()
        for i in range(2):
            wait_pair = pltpu.make_async_copy(arr0.at[:, :part], arr0.at[:, :part], bulk_sem.at[i])
            wait_pair.wait()
            others = pieces.at[pl.ds(0, group - 1), :part]
            pltpu.make_async_copy(others, others, scat_sem.at[i]).wait()

    @pl.when(off_diag)
    def _():
        for i in range(2):
            pltpu.make_async_copy(arr0, arr0, bulk_sem.at[i]).wait()
            others = pieces.at[pl.ds(0, group - 1)]
            pltpu.make_async_copy(others, others, scat_sem.at[i]).wait()


def second(n, size, k, flags, pieces, arr1, *scratch):
    pin, stage, outb = scratch[:3]
    slots = scratch[3:3 + SUBS]
    in_sem, mid_sem, dist_sem, own_sem = scratch[3 + SUBS:]
    b, d = lax.axis_index("bins"), lax.axis_index("diag")
    half, group = n // 2, size // B
    on_diag, off_diag = d == 0, d == 1
    partner = (lax.rem(b + half, n), d)
    place_in = lax.rem(b, group)
    base_chip = b - place_in

    def mate(off):
        return (base_chip + lax.rem(place_in + off, group), d)

    def run(tall):
        sub = tall // SUBS
        load = pltpu.make_async_copy(pieces.at[:, :tall], pin.at[:, :tall], in_sem.at[0])
        load.start()
        barrier = pltpu.get_barrier_semaphore()
        pl.semaphore_signal(barrier, inc=1, device_id=partner, device_id_type=MESH)
        for off in range(1, group):
            pl.semaphore_signal(barrier, inc=1, device_id=mate(off), device_id_type=MESH)

        ranks, before = [], jnp.int32(0)
        picks = [jnp.int32(0) for _ in range(k)]
        for p in range(group):
            flag = flags[p]
            for i in range(k):
                picks[i] = picks[i] + jnp.where(before == i, flag, 0) * p
            ranks.append(jnp.minimum(before, k - 1))
            before = before + flag
        load.wait()

        def mid(i, s):
            return pltpu.make_async_remote_copy(
                stage.at[i, pl.ds(s * sub, sub)], slots[s].at[i, :sub], mid_sem.at[0], mid_sem.at[1 + s], device_id=partner, device_id_type=MESH)

        for i in range(k):
            stage[i, :tall] = pin[picks[i], :tall]
        pl.semaphore_wait(barrier, group)
        for s in range(SUBS):
            for i in range(k):
                mid(i, s).start()

        for s in range(SUBS):
            rows = pl.ds(s * sub, sub)
            landed = slots[s].at[:, :sub]
            pltpu.make_async_copy(landed, landed, mid_sem.at[1 + s]).wait()
            for p in range(group):
                outb[p, s * sub:(s + 1) * sub] = slots[s][ranks[p], :sub]
            pltpu.make_async_copy(outb.at[place_in, rows], arr1.at[place_in, rows], own_sem.at[0]).start()

            def hand(off, carry):
                p = lax.rem(place_in + off, group)
                pltpu.make_async_remote_copy(
                    outb.at[p, rows], arr1.at[place_in, rows], dist_sem.at[0], dist_sem.at[1], device_id=(base_chip + p, d), device_id_type=MESH).start()
                return carry

            lax.fori_loop(1, group, hand, 0)

        sent = stage.at[:, :tall]
        pltpu.make_async_copy(sent, sent, mid_sem.at[0]).wait()
        mine = outb.at[0, :tall]
        pltpu.make_async_copy(mine, mine, own_sem.at[0]).wait()
        others = outb.at[pl.ds(0, group - 1), :tall]
        for i in range(2):
            pltpu.make_async_copy(others, others, dist_sem.at[i]).wait()

    @pl.when(on_diag)
    def _():
        run(B // 2)

    @pl.when(off_diag)
    def _():
        run(B)


def nothing(flags, arr1):
    del flags, arr1


def third(size, placed, u, v, diag, bias, arr0, arr1, held, out, bias_out, inb, outb, in_sem, out_sem):
    d = lax.axis_index("diag")
    strips = size // B
    part = B // 2
    bias_out[...] = bias[...]
    line = lax.broadcasted_iota(jnp.int32, (B, B), 0)
    lane = lax.broadcasted_iota(jnp.int32, (B, B), 1)
    arrs = (arr0, arr1)

    def rows_of(r):
        return pl.ds(pl.multiple_of(r * B, B), B)

    def write(t, r):
        return pltpu.make_async_copy(outb.at[t, r], out.at[t, 0, rows_of(r)], out_sem.at[t, r])

    def down(t, r):
        return jnp.broadcast_to(u[:, pl.ds(pl.multiple_of(t * size + r * B, B), B)], (B, B)).T

    def across(t, c):
        return v[:, t * size + c * B:t * size + (c + 1) * B]

    def folded_load(t, e):
        return pltpu.make_async_copy(arrs[t].at[e, :part], inb.at[t, e // 2, pl.ds((e % 2) * part, part)], in_sem.at[t, e])

    def home_load(t, r):
        return pltpu.make_async_copy(held.at[t, 0, rows_of(r)], inb.at[t, r], in_sem.at[t, r])

    def strip_load(t, r):
        return pltpu.make_async_copy(arrs[t].at[r], inb.at[t, r], in_sem.at[t, r])

    def loads(t, load):
        def go():
            for r in range(strips):
                load(t, r).start()
        return go

    def unfold(t):
        def go():
            for j in range(strips // 2):
                for e in (2 * j, 2 * j + 1):
                    folded_load(t, e).wait()
                fold = inb[t, j, :, :B]
                at = B
                for r in (j, strips - 1 - j):
                    scale = down(t, r)
                    for c in range(strips):
                        if c < r:
                            block = jnp.zeros((B, B), F32)
                        elif c == r and r == j:
                            block = jnp.where(line <= lane, fold, 0.0) * scale * across(t, c)
                        elif c == r:
                            corner = diag[:, t * size + c * B:t * size + (c + 1) * B]
                            block = jnp.where(line < lane, fold.T, jnp.where(line == lane, corner, 0.0)) * scale * across(t, c)
                        else:
                            block = inb[t, j, :, at:at + B] * scale * across(t, c)
                            at += B
                        outb[t, r, :, c * B:(c + 1) * B] = block
                    write(t, r).start()
        return go

    def straight(t, load, shift):
        def go():
            def step(r, carry):
                load(t, r).wait()
                scale = down(t, r)
                for c in range(strips):
                    block = inb[t, r, :, c * B:(c + 1) * B]
                    if shift is not None:
                        block = jnp.where(line + r * B <= lane + c * B, block, 0.0)
                    outb[t, r, :, c * B:(c + 1) * B] = block * scale * across(t, c)
                write(t, r).start()
                return carry

            lax.fori_loop(0, strips, step, 0)
        return go

    moved = placed[1] == 1
    stays = placed[1] != 1
    plans = [
        (d == 0, 0, folded_load, unfold(0)),
        (d == 1, 0, strip_load, straight(0, strip_load, None)),
        ((d == 0) & moved, 1, folded_load, unfold(1)),
        ((d == 1) & moved, 1, strip_load, straight(1, strip_load, None)),
        ((d == 0) & stays, 1, home_load, straight(1, home_load, 0)),
        ((d == 1) & stays, 1, home_load, straight(1, home_load, None)),
    ]
    for when, t, load, _ in plans:
        pl.when(when)(loads(t, load))
    for when, _, _, work in plans:
        pl.when(when)(work)
    for t in range(2):
        for r in range(strips):
            write(t, r).wait()


def local(n, held_tiles, placed, bin_mask, bias):
    rows_dev, size = held_tiles.shape[0], held_tiles.shape[2]
    strips, width, count = size // B, rows_dev * size, n * 2
    group = strips
    assert rows_dev == 2 and (n // 2) % group == 0
    vmem, anywhere, smem = (pl.BlockSpec(memory_space=space) for space in (pltpu.VMEM, pl.ANY, pltpu.SMEM))
    wide = jax.ShapeDtypeStruct((1, width), F32)
    store = jax.ShapeDtypeStruct((strips, B, size), F32)
    dma = pltpu.SemaphoreType.DMA
    vec, vec2 = pltpu.VMEM((1, width), F32), pltpu.VMEM((2, width), F32)
    half2 = pltpu.VMEM((2, size), F32)
    arr0, pieces, flags, u, v, bias_new, diag = pl.pallas_call(
        functools.partial(first, n, size),
        out_shape=(store, store, jax.ShapeDtypeStruct((group + 1,), jnp.int32), wide, wide, wide, wide),
        in_specs=[anywhere, smem, vmem, vmem],
        out_specs=(anywhere, anywhere, smem, vmem, vmem, vmem, vmem),
        scratch_shapes=[
            pltpu.VMEM((2, size, size), F32),
            pltpu.VMEM((2, strips // 2, B, size), F32),
            pltpu.VMEM((1, width), jnp.int32),
            pltpu.VMEM((2, 1, size), jnp.int32),
            vec2, vec2, half2, vec, vec, vec2, vec2, vec, vec, vec,
            pltpu.VMEM((2, 8, size), F32),
            vec, vec, vec,
            pltpu.VMEM((ITERS, 4, 2, width), F32),
            pltpu.VMEM((ITERS, 2, size), F32),
            pltpu.VMEM((ITERS, 2, 2, size), F32),
            pltpu.VMEM((ITERS, 2, size), F32),
            pltpu.VMEM((ITERS, 4, 2, size), F32),
            pltpu.VMEM((ITERS, count, 1, B), F32),
            vec,
            dma((2,)), dma((2,)), dma((4,)), dma((2,)), dma((2,)), dma((1,)), dma((2,)),
            dma((ITERS, 2)), dma((ITERS, 2)), dma((ITERS, 2)), dma((ITERS, 2)), dma((ITERS, 2)),
        ],
        compiler_params=pltpu.CompilerParams(collective_id=0, has_side_effects=True),
    )(held_tiles, placed, bin_mask.reshape(1, width), bias.reshape(1, width))

    def branch(k):
        if k == 0:
            return lambda flags, pieces: pl.pallas_call(
                nothing, out_shape=store, in_specs=[smem], out_specs=anywhere)(flags)
        sub = B // SUBS
        return lambda flags, pieces: pl.pallas_call(
            functools.partial(second, n, size, k),
            out_shape=store,
            in_specs=[smem, anywhere],
            out_specs=anywhere,
            scratch_shapes=[
                pltpu.VMEM((strips, B, size), F32),
                pltpu.VMEM((k, B, size), F32),
                pltpu.VMEM((strips, B, size), F32),
                *[pltpu.VMEM((k, sub, size), F32) for _ in range(SUBS)],
                dma((1,)), dma((1 + SUBS,)), dma((2,)), dma((1,)),
            ],
            compiler_params=pltpu.CompilerParams(collective_id=k, has_side_effects=True),
        )(flags, pieces)

    arr1 = lax.switch(flags[group], [branch(k) for k in range(group + 1)], flags, pieces)
    balanced, bias_new = pl.pallas_call(
        functools.partial(third, size),
        out_shape=(jax.ShapeDtypeStruct((rows_dev, 1, size, size), F32), wide),
        in_specs=[smem, vmem, vmem, vmem, vmem, anywhere, anywhere, anywhere],
        out_specs=(anywhere, vmem),
        scratch_shapes=[
            pltpu.VMEM((rows_dev, strips, B, size), F32),
            pltpu.VMEM((rows_dev, strips, B, size), F32),
            dma((rows_dev, strips)), dma((rows_dev, strips)),
        ],
    )(placed, u, v, diag, bias_new, arr0, arr1, held_tiles)
    return balanced, bias_new.reshape(width)


def solution(mesh):
    specs = (P("bins", "diag", None, None), P("bins"), P("bins"), P("bins"))
    return jax.shard_map(
        functools.partial(local, mesh.shape["bins"]),
        mesh=mesh,
        in_specs=specs,
        out_specs=(P("bins", "diag", None, None), P("bins")),
        check_vma=False,
    )
```

```python
import functools

import jax
import jax.numpy as jnp
from jax import lax
from jax.experimental import pallas as pl
from jax.experimental.pallas import tpu as pltpu
from jax.sharding import PartitionSpec as P

ITERS = 2
B = 128
SUBS = 8
EARLY = 4
MESH = pl.DeviceIdType.MESH
F32 = jnp.float32


def flip(place, mask):
    out, bit = 0, 1
    while bit <= mask:
        digit = lax.rem(place // bit, 2)
        out = out + bit * (1 - digit if mask & bit else digit)
        bit *= 2
    return out + place // bit * bit


def first(n, size, held, placed, mask, bias, arr0, pieces, flags_out, u_out, v_out, bias_out, diag_out,
          home, pack, p_mask, next_mask, live2, live_col2, nlive2, stored_row, stored_col, u2, v2, su, sv, row, col_acc, diag_vec, raw_vec, raw_in,
          quad, edge_out, edge_in, edge_pair, nxt, tot, sums_now,
          in_sem, mask_sem, nmask_sem, bulk_sem, scat_sem, own_sem, raw_sem, quad_sem, edge_sem, epair_sem, nxt_sem, tot_sem):
    b, d = lax.axis_index("bins"), lax.axis_index("diag")
    half = n // 2
    count = n * 2
    me = b * 2 + d
    on_diag, off_diag = d == 0, d == 1
    strips = size // B
    group = strips
    width = 2 * size
    part = B // 2
    side = b // half
    spot_l = lax.rem(b, half)
    partner = (lax.rem(b + half, n), d)
    slot = side * 2 + d
    prev_l, next_l = lax.rem(spot_l + half - 1, half), lax.rem(spot_l + 1, half)
    place_in = lax.rem(b, group)
    base_chip = b - place_in

    def remote(src, dst, send, recv, device):
        return pltpu.make_async_remote_copy(src, dst, send, recv, device_id=device, device_id_type=MESH)

    def other(off):
        target = lax.rem(me + off, count)
        return (target // 2, lax.rem(target, 2))

    barrier = pltpu.get_barrier_semaphore()

    def greet(off, carry):
        pl.semaphore_signal(barrier, inc=1, device_id=other(off), device_id_type=MESH)
        return carry

    lax.fori_loop(1, count, greet, 0)
    loads = []
    for t in range(2):
        loads.append(pltpu.make_async_copy(held.at[t, 0], home.at[t], in_sem.at[t]))
        loads[-1].start()
    pl.semaphore_wait(barrier, count - 1)

    mask_send = remote(mask, p_mask, mask_sem.at[0], mask_sem.at[1], partner)
    mask_send.start()
    nmask = [remote(mask.at[:, :size], next_mask.at[side], nmask_sem.at[i], nmask_sem.at[2 + side], (prev_l + i * half, 1)) for i in range(2)]

    @pl.when(on_diag)
    def _():
        for copy in nmask:
            copy.start()

    def rows_of(e, tall):
        return pl.ds(pl.multiple_of(e * tall, tall), tall)

    def bulk(e):
        diag_part = remote(pack.at[0, e // 2, pl.ds((e % 2) * part, part)], arr0.at[e, :part], bulk_sem.at[0], bulk_sem.at[1], partner)
        off_part = remote(held.at[0, 0, pl.ds(e * B, B)], arr0.at[e], bulk_sem.at[0], bulk_sem.at[1], partner)
        return diag_part, off_part

    def start_bulk(stage):
        @pl.when(on_diag)
        def _():
            for e in diag_cuts[stage]:
                bulk(e)[0].start()

        @pl.when(off_diag)
        def _():
            for e in off_cuts[stage]:
                bulk(e)[1].start()

    def start_scatter(off):
        e = flip(place_in, off)

        @pl.when(on_diag)
        def _():
            remote(pack.at[1, e // 2, rows_of(lax.rem(e, 2), part)], pieces.at[place_in, :part], scat_sem.at[0], scat_sem.at[1], (base_chip + e, d)).start()

        @pl.when(off_diag)
        def _():
            remote(held.at[1, 0, rows_of(e, B)], pieces.at[place_in], scat_sem.at[0], scat_sem.at[1], (base_chip + e, d)).start()

    line = lax.broadcasted_iota(jnp.int32, (B, B), 0)
    lane = lax.broadcasted_iota(jnp.int32, (B, B), 1)

    def fold_tile(t):
        for j in range(strips // 2):
            k = strips - 1 - j
            low, high = home[t, j * B:(j + 1) * B, j * B:(j + 1) * B], home[t, k * B:(k + 1) * B, k * B:(k + 1) * B]
            pack[t, j, :, :B] = jnp.where(line <= lane, low, high.T)
            mid = (strips - j) * B
            pack[t, j, :, B:mid] = home[t, j * B:(j + 1) * B, (j + 1) * B:]
            if mid < size:
                pack[t, j, :, mid:] = home[t, k * B:(k + 1) * B, (k + 1) * B:]

            for q, block in ((j, low), (k, high)):
                raw_vec[:, t * size + q * B:t * size + (q + 1) * B] = jnp.sum(jnp.where(line == lane, block, 0.0), axis=0, keepdims=True)

    own_off = pltpu.make_async_copy(home.at[1, rows_of(place_in, B)], pieces.at[place_in], own_sem.at[0])
    own_diag = pltpu.make_async_copy(pack.at[1, place_in // 2, rows_of(lax.rem(place_in, 2), part)], pieces.at[place_in, :part], own_sem.at[0])
    raw_send = remote(raw_vec, raw_in, raw_sem.at[0], raw_sem.at[1], partner)

    diag_cuts = (range(0, 0), range(0, 1), range(1, 8))
    off_cuts = (range(0, 2), range(2, 3), range(3, 4))

    @pl.when(off_diag)
    def _():
        for e in off_cuts[0]:
            bulk(e)[1].start()

    for t in range(2):
        loads[t].wait()

    @pl.when(on_diag)
    def _():
        fold_tile(0)
        for e in diag_cuts[0]:
            bulk(e)[0].start()
        fold_tile(1)
        own_diag.start()
        raw_send.start()

    @pl.when(off_diag)
    def _():
        own_off.start()

    mask_send.wait()

    @pl.when(off_diag)
    def _():
        for i in range(2):
            remote(mask.at[:, :size], next_mask.at[i], nmask_sem.at[0], nmask_sem.at[2 + i], partner).wait_recv()

    @pl.when(on_diag)
    def _():
        for copy in nmask:
            copy.wait_send()

    def pair_of(own, their):
        lower, upper = jnp.where(side == 0, own, their), jnp.where(side == 0, their, own)
        return jnp.concatenate([lower, upper], axis=0)

    def own_of(both):
        return jnp.where(side == 0, both[0:1], both[1:2])

    flag = jnp.full((1, size), placed[1]) == 1
    gone = jnp.concatenate([jnp.ones((1, size), jnp.int32), flag.astype(jnp.int32)], axis=1)
    at_side = jnp.where(gone == 1, 1 - side, side)

    def stored(both):
        return jnp.where(at_side == 0, both[0:1], both[1:2])

    sides = lax.broadcasted_iota(jnp.int32, (2, width), 0)

    def put_home(vector):
        return jnp.where(sides == at_side, vector, 0.0)

    def from_next(both):
        return jnp.where(spot_l == half - 1, jnp.concatenate([both[1:2], jnp.zeros_like(both[0:1])], axis=0), both)

    def from_prev(both):
        return jnp.where(spot_l == 0, jnp.concatenate([jnp.zeros_like(both[0:1]), both[0:1]], axis=0), both)

    live2[...] = pair_of(mask[...].astype(F32), p_mask[...].astype(F32))
    nlive2[...] = jnp.zeros_like(nlive2)

    @pl.when(off_diag)
    def _():
        nlive2[...] = from_next(jnp.concatenate([next_mask[0], next_mask[1]], axis=0).astype(F32))

    live_col2[...] = jnp.where(on_diag, live2[...], jnp.concatenate([live2[:, size:], nlive2[...]], axis=1))
    stored_row[...] = stored(live2[...])
    stored_col[...] = stored(live_col2[...])
    u2[...] = jnp.ones_like(u2)
    v2[...] = jnp.ones_like(v2)
    su[...] = jnp.ones_like(su)
    sv[...] = jnp.ones_like(sv)
    bias_out[...] = bias[...]
    shift = jnp.where(on_diag, 0, -2 * size)

    def down(vector):
        return jnp.broadcast_to(vector, (B, B)).T

    def folded(block):
        return jnp.sum(block.reshape(B // 8, 8, B), axis=0)

    first_lane = lax.broadcasted_iota(jnp.int32, (1, B), 1)

    def settle(k):
        many = tot.at[k, pl.ds(0, count - 1)]
        pltpu.make_async_copy(many, many, tot_sem.at[k, 0]).wait()
        pltpu.make_async_copy(many, many, tot_sem.at[k, 1]).wait()
        both = jnp.sum(tot[k], axis=0)
        mean = jnp.sum(jnp.where(first_lane == 0, both, 0.0), axis=1, keepdims=True) / jnp.sum(
            jnp.where(first_lane == 1, both, 0.0), axis=1, keepdims=True)
        bias_out[...] = bias_out[...] * jnp.where(mask[...] > 0, sums_now[...] / mean, 1.0)
        u2[...] = u2[...] * jnp.where(live2[...] > 0, mean, 1.0)
        v2[...] = v2[...] * jnp.where(live_col2[...] > 0, mean, 1.0)
        return mean

    for k in range(ITERS):
        col_acc[...] = jnp.zeros_like(col_acc)
        for t in range(2):
            if k == 0 and t == 1:
                @pl.when(off_diag)
                def _():
                    own_off.wait()

            def strip_pass(r, carry):
                rows = rows_of(r, B)
                spot = pl.ds(pl.multiple_of(t * size + r * B, B), B)
                total = jnp.zeros((B, B), F32)
                if k == 0:
                    live_down = down(stored_row[:, spot])
                    for c in range(strips):
                        block = home[t, rows, c * B:(c + 1) * B]
                        keep = line + (r * B + shift) <= lane + c * B
                        block = jnp.where(keep, block, 0.0) * live_down * stored_col[:, t * size + c * B:t * size + (c + 1) * B]
                        home[t, rows, c * B:(c + 1) * B] = block
                        col_acc[t, :, c * B:(c + 1) * B] += folded(block)
                        total = total + block
                    corner = home[t, rows, rows]
                    diag_vec[:, spot] = jnp.where(on_diag, jnp.sum(jnp.where(line == lane, corner, 0.0), axis=0, keepdims=True), 0.0)
                else:
                    u_down = down(su[:, spot])
                    for c in range(strips):
                        block = home[t, rows, c * B:(c + 1) * B]
                        col_acc[t, :, c * B:(c + 1) * B] += folded(block * u_down)
                        total = total + block * sv[:, t * size + c * B:t * size + (c + 1) * B]
                row[:, spot] = jnp.sum(total.T, axis=0, keepdims=True)
                return carry

            lax.fori_loop(0, strips, strip_pass, 0)

        cols = jnp.concatenate([jnp.sum(col_acc[t], axis=0, keepdims=True) for t in range(2)], axis=1) * sv[...]
        rows2 = put_home(row[...] * su[...])
        corner2 = put_home(diag_vec[...] * su[...] * sv[...])
        cols2 = put_home(cols)
        zero = jnp.zeros((2, size), F32)
        mine = rows2 + jnp.where(on_diag, cols2 - corner2, jnp.concatenate([zero, cols2[:, :size]], axis=1))
        edge = jnp.where(on_diag, 0.0, cols2[:, size:])
        if k > 0:
            mean = settle(k - 1)
            mine, edge = (jnp.where(value != 0, value * mean * mean, 0.0) for value in (mine, edge))
        quad[k, slot] = mine
        edge_out[k] = edge
        partial = jnp.sum(mine) + jnp.sum(edge)
        kept = jnp.where(on_diag, jnp.sum(mask[...].astype(F32)), 0.0)
        marked = jnp.full((1, B), placed[1]).astype(F32)
        tot[k, me] = jnp.where(first_lane == 0, partial, jnp.where(first_lane == 1, kept, jnp.where(first_lane == 2, marked, 0.0)))

        def quad_copy(off):
            q = lax.rem(slot + off, 4)
            return remote(quad.at[k, slot], quad.at[k, slot], quad_sem.at[k, 0], quad_sem.at[k, 1], (spot_l + (q // 2) * half, lax.rem(q, 2)))

        nxt_copies = [remote(quad.at[k, slot, :, :size], nxt.at[k, slot], nxt_sem.at[k, 0], nxt_sem.at[k, 1], (prev_l + i * half, 1)) for i in range(2)]
        edge_copies = [remote(edge_out.at[k], edge_in.at[k, side], edge_sem.at[k, 0], edge_sem.at[k, 1], (next_l + (i // 2) * half, i % 2)) for i in range(4)]
        epair = remote(edge_out.at[k], edge_pair.at[k], epair_sem.at[k, 0], epair_sem.at[k, 1], partner)

        for off in range(1, 4):
            quad_copy(off).start()
        for copy in nxt_copies:
            copy.start()

        @pl.when(off_diag)
        def _():
            for copy in edge_copies:
                copy.start()
            epair.start()

        def tot_start(off, carry):
            remote(tot.at[k, me], tot.at[k, me], tot_sem.at[k, 0], tot_sem.at[k, 1], other(off)).start()
            return carry

        lax.fori_loop(1, count, tot_start, 0)

        if k == 0:
            for off in range(1, group):
                start_scatter(off)
            start_bulk(1)
        else:
            start_bulk(2)

        def wait_all(ref, sem):
            pltpu.make_async_copy(ref, ref, sem).wait()

        wait_all(quad.at[k, pl.ds(0, 3)], quad_sem.at[k, 1])
        wait_all(edge_in.at[k], edge_sem.at[k, 1])

        @pl.when(off_diag)
        def _():
            wait_all(nxt.at[k], nxt_sem.at[k, 1])
            epair.wait_recv()

        wait_all(quad.at[k, pl.ds(0, 3)], quad_sem.at[k, 0])
        wait_all(nxt.at[k, pl.ds(0, 2)], nxt_sem.at[k, 0])

        @pl.when(off_diag)
        def _():
            wait_all(edge_in.at[k], edge_sem.at[k, 0])
            wait_all(edge_in.at[k], edge_sem.at[k, 0])
            epair.wait_send()

        sums = (quad[k, 0] + quad[k, 1]) + (quad[k, 2] + quad[k, 3])
        arrived = from_prev(edge_in[k, 0] + edge_in[k, 1])
        sums = sums + jnp.concatenate([arrived, jnp.zeros((2, size), F32)], axis=1)
        sums_now[...] = own_of(sums)
        inverse = 1.0 / jnp.where(live2[...] > 0, sums, 1.0)
        u2[...] = u2[...] * inverse

        @pl.when(on_diag)
        def _():
            v2[...] = v2[...] * inverse

        @pl.when(off_diag)
        def _():
            next_sums = from_next((nxt[k, 0] + nxt[k, 1]) + (nxt[k, 2] + nxt[k, 3])) + (edge_out[k] + edge_pair[k])
            next_inverse = 1.0 / jnp.where(nlive2[...] > 0, next_sums, 1.0)
            v2[...] = v2[...] * jnp.concatenate([inverse[:, size:], next_inverse], axis=1)

        su[...] = stored(u2[...])
        sv[...] = stored(v2[...])

    settle(ITERS - 1)
    u_out[...] = own_of(jnp.where(live2[...] > 0, u2[...], 0.0))
    v_out[...] = own_of(jnp.where(live_col2[...] > 0, v2[...], 0.0))

    best = None
    for g in range(half // group):
        several = tot[0, g * group * 2]
        for p in range(1, group):
            several = several + tot[0, (g * group + p) * 2]
        best = several if best is None else jnp.maximum(best, several)
    flags_out[group] = jnp.sum(jnp.where(first_lane == 2, best, 0.0)).astype(jnp.int32)
    for p in range(group):
        flags_out[p] = jnp.sum(jnp.where(first_lane == 2, tot[0, (base_chip + p) * 2], 0.0)).astype(jnp.int32)

    diag_out[...] = jnp.zeros_like(diag_out)

    @pl.when(on_diag)
    def _():
        raw_send.wait()
        diag_out[...] = jnp.where(gone == 1, raw_in[...], raw_vec[...])
        own_diag.wait()
        for i in range(2):
            wait_pair = pltpu.make_async_copy(arr0.at[:, :part], arr0.at[:, :part], bulk_sem.at[i])
            wait_pair.wait()
            others = pieces.at[pl.ds(0, group - 1), :part]
            pltpu.make_async_copy(others, others, scat_sem.at[i]).wait()

    @pl.when(off_diag)
    def _():
        for i in range(2):
            sent = arr0.at[pl.ds(0, EARLY)]
            pltpu.make_async_copy(sent, sent, bulk_sem.at[i]).wait()
            others = pieces.at[pl.ds(0, group - 1)]
            pltpu.make_async_copy(others, others, scat_sem.at[i]).wait()


def second(n, size, k, flags, pieces, held, arr1, rest, *scratch):
    pin, stage, outb = scratch[:3]
    slots = scratch[3:3 + SUBS]
    in_sem, mid_sem, dist_sem, own_sem, rest_sem = scratch[3 + SUBS:]
    b, d = lax.axis_index("bins"), lax.axis_index("diag")
    half, group = n // 2, size // B
    strips = size // B
    on_diag, off_diag = d == 0, d == 1
    partner = (lax.rem(b + half, n), d)
    place_in = lax.rem(b, group)
    base_chip = b - place_in

    def mate(off):
        return (base_chip + flip(place_in, off), d)

    def send_rest(first, last):
        for r in range(first, last):
            pltpu.make_async_remote_copy(
                held.at[0, 0, pl.ds(r * B, B)], rest.at[r - EARLY], rest_sem.at[0], rest_sem.at[1], device_id=partner, device_id_type=MESH).start()

    def run(tall, has_rest):
        sub = tall // SUBS
        if k > 0:
            load = pltpu.make_async_copy(pieces.at[:, :tall], pin.at[:, :tall], in_sem.at[0])
            load.start()
        barrier = pltpu.get_barrier_semaphore()
        pl.semaphore_signal(barrier, inc=1, device_id=partner, device_id_type=MESH)
        for off in range(1, group):
            pl.semaphore_signal(barrier, inc=1, device_id=mate(off), device_id_type=MESH)

        def mid(i, s):
            return pltpu.make_async_remote_copy(
                stage.at[i, pl.ds(s * sub, sub)], slots[s].at[i, :sub], mid_sem.at[0], mid_sem.at[1 + s], device_id=partner, device_id_type=MESH)

        if k > 0:
            ranks, before = [], jnp.int32(0)
            picks = [jnp.int32(0) for _ in range(k)]
            for p in range(group):
                flag = flags[p]
                for i in range(k):
                    picks[i] = picks[i] + jnp.where(before == i, flag, 0) * p
                ranks.append(jnp.minimum(before, k - 1))
                before = before + flag
            load.wait()
            for i in range(k):
                stage[i, :tall] = pin[picks[i], :tall]
        pl.semaphore_wait(barrier, group)
        if k > 0:
            for s in range(SUBS):
                for i in range(k):
                    mid(i, s).start()
            for s in range(SUBS):
                if has_rest and s == SUBS // 2:
                    send_rest(EARLY, EARLY + 1)
                rows = pl.ds(s * sub, sub)
                landed = slots[s].at[:, :sub]
                pltpu.make_async_copy(landed, landed, mid_sem.at[1 + s]).wait()
                for p in range(group):
                    outb[p, s * sub:(s + 1) * sub] = slots[s][ranks[p], :sub]
                pltpu.make_async_copy(outb.at[place_in, rows], arr1.at[place_in, rows], own_sem.at[0]).start()
                for off in range(1, group):
                    pltpu.make_async_remote_copy(
                        outb.at[flip(place_in, off), rows], arr1.at[place_in, rows], dist_sem.at[0], dist_sem.at[1],
                        device_id=mate(off), device_id_type=MESH).start()
        if has_rest:
            send_rest(EARLY + 1 if k > 0 else EARLY, strips)
        if k > 0:
            sent = stage.at[:, :tall]
            pltpu.make_async_copy(sent, sent, mid_sem.at[0]).wait()
            mine = outb.at[0, :tall]
            pltpu.make_async_copy(mine, mine, own_sem.at[0]).wait()
            others = outb.at[pl.ds(0, group - 1), :tall]
            for i in range(2):
                pltpu.make_async_copy(others, others, dist_sem.at[i]).wait()
        if has_rest:
            for i in range(2):
                pltpu.make_async_copy(rest, rest, rest_sem.at[i]).wait()

    @pl.when(on_diag)
    def _():
        run(B // 2, False)

    @pl.when(off_diag)
    def _():
        run(B, True)


def scaled(size, u, v, diag, out, inb, outb, in_sem, out_sem):
    strips = size // B
    part = B // 2
    line = lax.broadcasted_iota(jnp.int32, (B, B), 0)
    lane = lax.broadcasted_iota(jnp.int32, (B, B), 1)

    def rows_of(r):
        return pl.ds(pl.multiple_of(r * B, B), B)

    def down(t, r):
        return jnp.broadcast_to(u[:, pl.ds(pl.multiple_of(t * size + r * B, B), B)], (B, B)).T

    def across(t, c):
        return v[:, t * size + c * B:t * size + (c + 1) * B]

    def write(t, r, at):
        return pltpu.make_async_copy(outb.at[at], out.at[t, 0, rows_of(r)], out_sem.at[at])

    def unfold(t, arr):
        def load(e):
            return pltpu.make_async_copy(arr.at[e, :part], inb.at[e // 2, pl.ds((e % 2) * part, part)], in_sem.at[e])

        for e in range(strips):
            load(e).start()
        for j in range(strips // 2):
            for e in (2 * j, 2 * j + 1):
                load(e).wait()
            fold = inb[j, :, :B]
            at = B
            for r in (j, strips - 1 - j):
                scale = down(t, r)
                for c in range(strips):
                    if c < r:
                        block = jnp.zeros((B, B), F32)
                    elif c == r and r == j:
                        block = jnp.where(line <= lane, fold, 0.0) * scale * across(t, c)
                    elif c == r:
                        corner = diag[:, t * size + c * B:t * size + (c + 1) * B]
                        block = jnp.where(line < lane, fold.T, jnp.where(line == lane, corner, 0.0)) * scale * across(t, c)
                    else:
                        block = inb[j, :, at:at + B] * scale * across(t, c)
                        at += B
                    outb[r, :, c * B:(c + 1) * B] = block
                write(t, r, r).start()
        for r in range(strips):
            write(t, r, r).wait()

    def straight(jobs, cut=False):
        def load(source, r, at):
            return pltpu.make_async_copy(source(r), inb.at[at], in_sem.at[at])

        for t, source, first, last, base in jobs:
            for r in range(first, last):
                load(source, r, base + r).start()
        for t, source, first, last, base in jobs:
            def step(r, carry):
                at = base + r
                load(source, r, at).wait()
                scale = down(t, r)
                for c in range(strips):
                    block = inb[at, :, c * B:(c + 1) * B]
                    if cut:
                        block = jnp.where(line + r * B <= lane + c * B, block, 0.0)
                    outb[at, :, c * B:(c + 1) * B] = block * scale * across(t, c)
                write(t, r, at).start()
                return carry

            lax.fori_loop(first, last, step, 0)
        for t, source, first, last, base in jobs:
            for r in range(first, last):
                write(t, r, base + r).wait()

    return rows_of, unfold, straight


def third(size, u, v, diag, arr0, out, *scratch):
    d = lax.axis_index("diag")
    _, unfold, straight = scaled(size, u, v, diag, out, *scratch)

    @pl.when(d == 0)
    def _():
        unfold(0, arr0)

    @pl.when(d == 1)
    def _():
        straight([(0, lambda r: arr0.at[r], 0, EARLY, 0)])


def fourth(size, placed, u, v, diag, bias, arr1, rest, held, done, out, bias_out, *scratch):
    del done
    d = lax.axis_index("diag")
    strips = size // B
    bias_out[...] = bias[...]
    rows_of, unfold, straight = scaled(size, u, v, diag, out, *scratch)
    moved, stays = placed[1] == 1, placed[1] != 1
    late = (0, lambda r: rest.at[r - EARLY], EARLY, strips, strips - EARLY)

    @pl.when((d == 0) & moved)
    def _():
        unfold(1, arr1)

    @pl.when((d == 1) & moved)
    def _():
        straight([(1, lambda r: arr1.at[r], 0, strips, 0), late])

    @pl.when((d == 0) & stays)
    def _():
        straight([(1, lambda r: held.at[1, 0, rows_of(r)], 0, strips, 0)], cut=True)

    @pl.when((d == 1) & stays)
    def _():
        straight([(1, lambda r: held.at[1, 0, rows_of(r)], 0, strips, 0), late])


def local(n, held_tiles, placed, bin_mask, bias):
    rows_dev, size = held_tiles.shape[0], held_tiles.shape[2]
    strips, width, count = size // B, rows_dev * size, n * 2
    group = strips
    assert rows_dev == 2 and (n // 2) % group == 0
    vmem, anywhere, smem = (pl.BlockSpec(memory_space=space) for space in (pltpu.VMEM, pl.ANY, pltpu.SMEM))
    wide = jax.ShapeDtypeStruct((1, width), F32)
    store = jax.ShapeDtypeStruct((strips, B, size), F32)
    dma = pltpu.SemaphoreType.DMA
    vec, vec2 = pltpu.VMEM((1, width), F32), pltpu.VMEM((2, width), F32)
    half2 = pltpu.VMEM((2, size), F32)
    arr0, pieces, flags, u, v, bias_new, diag = pl.pallas_call(
        functools.partial(first, n, size),
        out_shape=(store, store, jax.ShapeDtypeStruct((group + 1,), jnp.int32), wide, wide, wide, wide),
        in_specs=[anywhere, smem, vmem, vmem],
        out_specs=(anywhere, anywhere, smem, vmem, vmem, vmem, vmem),
        scratch_shapes=[
            pltpu.VMEM((2, size, size), F32),
            pltpu.VMEM((2, strips // 2, B, size), F32),
            pltpu.VMEM((1, width), jnp.int32),
            pltpu.VMEM((2, 1, size), jnp.int32),
            vec2, vec2, half2, vec, vec, vec2, vec2, vec, vec, vec,
            pltpu.VMEM((2, 8, size), F32),
            vec, vec, vec,
            pltpu.VMEM((ITERS, 4, 2, width), F32),
            pltpu.VMEM((ITERS, 2, size), F32),
            pltpu.VMEM((ITERS, 2, 2, size), F32),
            pltpu.VMEM((ITERS, 2, size), F32),
            pltpu.VMEM((ITERS, 4, 2, size), F32),
            pltpu.VMEM((ITERS, count, 1, B), F32),
            vec,
            dma((2,)), dma((2,)), dma((4,)), dma((2,)), dma((2,)), dma((1,)), dma((2,)),
            dma((ITERS, 2)), dma((ITERS, 2)), dma((ITERS, 2)), dma((ITERS, 2)), dma((ITERS, 2)),
        ],
        compiler_params=pltpu.CompilerParams(collective_id=0, has_side_effects=True),
    )(held_tiles, placed, bin_mask.reshape(1, width), bias.reshape(1, width))

    left = strips - EARLY
    remain = jax.ShapeDtypeStruct((left, B, size), F32)

    def branch(k):
        sub, most = B // SUBS, max(k, 1)
        return lambda flags, pieces, held: pl.pallas_call(
            functools.partial(second, n, size, k),
            out_shape=(store, remain),
            in_specs=[smem, anywhere, anywhere],
            out_specs=(anywhere, anywhere),
            scratch_shapes=[
                pltpu.VMEM((strips, B, size), F32),
                pltpu.VMEM((most, B, size), F32),
                pltpu.VMEM((strips, B, size), F32),
                *[pltpu.VMEM((most, sub, size), F32) for _ in range(SUBS)],
                dma((1,)), dma((1 + SUBS,)), dma((2,)), dma((1,)), dma((2,)),
            ],
            compiler_params=pltpu.CompilerParams(collective_id=1 + k, has_side_effects=True),
        )(flags, pieces, held)

    whole = jax.ShapeDtypeStruct((rows_dev, 1, size, size), F32)

    def strip_scratch(slots):
        return [pltpu.VMEM((slots, B, size), F32), pltpu.VMEM((slots, B, size), F32), dma((slots,)), dma((slots,))]

    balanced = pl.pallas_call(
        functools.partial(third, size),
        out_shape=whole,
        in_specs=[vmem, vmem, vmem, anywhere],
        out_specs=anywhere,
        scratch_shapes=strip_scratch(strips),
    )(u, v, diag, arr0)
    flags, balanced = lax.optimization_barrier((flags, balanced))
    arr1, rest = lax.switch(flags[group], [branch(k) for k in range(group + 1)], flags, pieces, held_tiles)
    balanced, bias_new = pl.pallas_call(
        functools.partial(fourth, size),
        out_shape=(whole, wide),
        in_specs=[smem, vmem, vmem, vmem, vmem, anywhere, anywhere, anywhere, anywhere],
        out_specs=(anywhere, vmem),
        scratch_shapes=strip_scratch(strips + left),
        input_output_aliases={8: 0},
    )(placed, u, v, diag, bias_new, arr1, rest, held_tiles, balanced)
    return balanced, bias_new.reshape(width)


def solution(mesh):
    specs = (P("bins", "diag", None, None), P("bins"), P("bins"), P("bins"))
    return jax.shard_map(
        functools.partial(local, mesh.shape["bins"]),
        mesh=mesh,
        in_specs=specs,
        out_specs=(P("bins", "diag", None, None), P("bins")),
        check_vma=False,
    )
```

```python
import functools

import jax
import jax.numpy as jnp
from jax import lax
from jax.experimental import pallas as pl
from jax.experimental.pallas import tpu as pltpu
from jax.sharding import PartitionSpec as P

ITERS = 2
B = 128
SUBS = 8
GRANT = 52 << 20
MESH = pl.DeviceIdType.MESH
F32 = jnp.float32


def early_of(size):
    return size // B // 2


def flip(place, mask):
    out, bit = 0, 1
    while bit <= mask:
        digit = lax.rem(place // bit, 2)
        out = out + bit * (1 - digit if mask & bit else digit)
        bit *= 2
    return out + place // bit * bit


def first(n, size, held, placed, mask, bias, arr0, pieces, flags_out, u_out, v_out, bias_out, diag_out,
          home, pack, p_mask, next_mask, live2, live_col2, nlive2, stored_row, stored_col, u2, v2, su, sv, row, col_acc, diag_vec, raw_vec, raw_in,
          quad, edge_out, edge_in, edge_pair, nxt, tot, sums_now,
          in_sem, mask_sem, nmask_sem, bulk_sem, scat_sem, own_sem, raw_sem, quad_sem, edge_sem, epair_sem, nxt_sem, tot_sem):
    b, d = lax.axis_index("bins"), lax.axis_index("diag")
    half = n // 2
    count = n * 2
    me = b * 2 + d
    on_diag, off_diag = d == 0, d == 1
    strips = size // B
    group = strips
    width = 2 * size
    part = B // 2
    side = b // half
    spot_l = lax.rem(b, half)
    partner = (lax.rem(b + half, n), d)
    slot = side * 2 + d
    prev_l, next_l = lax.rem(spot_l + half - 1, half), lax.rem(spot_l + 1, half)
    place_in = lax.rem(b, group)
    base_chip = b - place_in

    def remote(src, dst, send, recv, device):
        return pltpu.make_async_remote_copy(src, dst, send, recv, device_id=device, device_id_type=MESH)

    def other(off):
        target = lax.rem(me + off, count)
        return (target // 2, lax.rem(target, 2))

    barrier = pltpu.get_barrier_semaphore()

    def greet(off, carry):
        pl.semaphore_signal(barrier, inc=1, device_id=other(off), device_id_type=MESH)
        return carry

    lax.fori_loop(1, count, greet, 0)
    loads = []
    for t in range(2):
        loads.append(pltpu.make_async_copy(held.at[t, 0], home.at[t], in_sem.at[t]))
        loads[-1].start()
    pl.semaphore_wait(barrier, count - 1)

    mask_send = remote(mask, p_mask, mask_sem.at[0], mask_sem.at[1], partner)
    mask_send.start()
    nmask = [remote(mask.at[:, :size], next_mask.at[side], nmask_sem.at[i], nmask_sem.at[2 + side], (prev_l + i * half, 1)) for i in range(2)]

    @pl.when(on_diag)
    def _():
        for copy in nmask:
            copy.start()

    def rows_of(e, tall):
        return pl.ds(pl.multiple_of(e * tall, tall), tall)

    def bulk(e):
        diag_part = remote(pack.at[0, e // 2, pl.ds((e % 2) * part, part)], arr0.at[e, :part], bulk_sem.at[0], bulk_sem.at[1], partner)
        off_part = remote(held.at[0, 0, pl.ds(e * B, B)], arr0.at[e], bulk_sem.at[0], bulk_sem.at[1], partner)
        return diag_part, off_part

    def start_bulk(stage):
        @pl.when(on_diag)
        def _():
            for e in diag_cuts[stage]:
                bulk(e)[0].start()

        @pl.when(off_diag)
        def _():
            for e in off_cuts[stage]:
                bulk(e)[1].start()

    def start_scatter(off):
        e = flip(place_in, off)

        @pl.when(on_diag)
        def _():
            remote(pack.at[1, e // 2, rows_of(lax.rem(e, 2), part)], pieces.at[place_in, :part], scat_sem.at[0], scat_sem.at[1], (base_chip + e, d)).start()

        @pl.when(off_diag)
        def _():
            remote(held.at[1, 0, rows_of(e, B)], pieces.at[place_in], scat_sem.at[0], scat_sem.at[1], (base_chip + e, d)).start()

    line = lax.broadcasted_iota(jnp.int32, (B, B), 0)
    lane = lax.broadcasted_iota(jnp.int32, (B, B), 1)

    def fold_tile(t):
        for j in range(strips // 2):
            k = strips - 1 - j
            low, high = home[t, j * B:(j + 1) * B, j * B:(j + 1) * B], home[t, k * B:(k + 1) * B, k * B:(k + 1) * B]
            pack[t, j, :, :B] = jnp.where(line <= lane, low, high.T)
            mid = (strips - j) * B
            pack[t, j, :, B:mid] = home[t, j * B:(j + 1) * B, (j + 1) * B:]
            if mid < size:
                pack[t, j, :, mid:] = home[t, k * B:(k + 1) * B, (k + 1) * B:]

            for q, block in ((j, low), (k, high)):
                raw_vec[:, t * size + q * B:t * size + (q + 1) * B] = jnp.sum(jnp.where(line == lane, block, 0.0), axis=0, keepdims=True)

    own_off = pltpu.make_async_copy(home.at[1, rows_of(place_in, B)], pieces.at[place_in], own_sem.at[0])
    own_diag = pltpu.make_async_copy(pack.at[1, place_in // 2, rows_of(lax.rem(place_in, 2), part)], pieces.at[place_in, :part], own_sem.at[0])
    raw_send = remote(raw_vec, raw_in, raw_sem.at[0], raw_sem.at[1], partner)

    diag_cuts = (range(0), range(1), range(1, strips))
    off_cuts = (range(early_of(size) - 2), range(early_of(size) - 2, early_of(size) - 1), range(early_of(size) - 1, early_of(size)))

    @pl.when(off_diag)
    def _():
        for e in off_cuts[0]:
            bulk(e)[1].start()

    for t in range(2):
        loads[t].wait()

    @pl.when(on_diag)
    def _():
        fold_tile(0)
        for e in diag_cuts[0]:
            bulk(e)[0].start()
        fold_tile(1)
        own_diag.start()
        raw_send.start()

    @pl.when(off_diag)
    def _():
        own_off.start()

    mask_send.wait()

    @pl.when(off_diag)
    def _():
        for i in range(2):
            remote(mask.at[:, :size], next_mask.at[i], nmask_sem.at[0], nmask_sem.at[2 + i], partner).wait_recv()

    @pl.when(on_diag)
    def _():
        for copy in nmask:
            copy.wait_send()

    def pair_of(own, their):
        lower, upper = jnp.where(side == 0, own, their), jnp.where(side == 0, their, own)
        return jnp.concatenate([lower, upper], axis=0)

    def own_of(both):
        return jnp.where(side == 0, both[0:1], both[1:2])

    flag = jnp.full((1, size), placed[1]) == 1
    gone = jnp.concatenate([jnp.ones((1, size), jnp.int32), flag.astype(jnp.int32)], axis=1)
    at_side = jnp.where(gone == 1, 1 - side, side)

    def stored(both):
        return jnp.where(at_side == 0, both[0:1], both[1:2])

    sides = lax.broadcasted_iota(jnp.int32, (2, width), 0)

    def put_home(vector):
        return jnp.where(sides == at_side, vector, 0.0)

    def from_next(both):
        return jnp.where(spot_l == half - 1, jnp.concatenate([both[1:2], jnp.zeros_like(both[0:1])], axis=0), both)

    def from_prev(both):
        return jnp.where(spot_l == 0, jnp.concatenate([jnp.zeros_like(both[0:1]), both[0:1]], axis=0), both)

    live2[...] = pair_of(mask[...].astype(F32), p_mask[...].astype(F32))
    nlive2[...] = jnp.zeros_like(nlive2)

    @pl.when(off_diag)
    def _():
        nlive2[...] = from_next(jnp.concatenate([next_mask[0], next_mask[1]], axis=0).astype(F32))

    live_col2[...] = jnp.where(on_diag, live2[...], jnp.concatenate([live2[:, size:], nlive2[...]], axis=1))
    stored_row[...] = stored(live2[...])
    stored_col[...] = stored(live_col2[...])
    u2[...] = jnp.ones_like(u2)
    v2[...] = jnp.ones_like(v2)
    su[...] = jnp.ones_like(su)
    sv[...] = jnp.ones_like(sv)
    bias_out[...] = bias[...]
    shift = jnp.where(on_diag, 0, -2 * size)

    def down(vector):
        return jnp.broadcast_to(vector, (B, B)).T

    def folded(block):
        return jnp.sum(block.reshape(B // 8, 8, B), axis=0)

    first_lane = lax.broadcasted_iota(jnp.int32, (1, B), 1)

    def settle(k):
        many = tot.at[k, pl.ds(0, count - 1)]
        pltpu.make_async_copy(many, many, tot_sem.at[k, 0]).wait()
        pltpu.make_async_copy(many, many, tot_sem.at[k, 1]).wait()
        both = jnp.sum(tot[k], axis=0)
        mean = jnp.sum(jnp.where(first_lane == 0, both, 0.0), axis=1, keepdims=True) / jnp.sum(
            jnp.where(first_lane == 1, both, 0.0), axis=1, keepdims=True)
        bias_out[...] = bias_out[...] * jnp.where(mask[...] > 0, sums_now[...] / mean, 1.0)
        u2[...] = u2[...] * jnp.where(live2[...] > 0, mean, 1.0)
        v2[...] = v2[...] * jnp.where(live_col2[...] > 0, mean, 1.0)
        return mean

    for k in range(ITERS):
        col_acc[...] = jnp.zeros_like(col_acc)
        for t in range(2):
            if k == 0 and t == 1:
                @pl.when(off_diag)
                def _():
                    own_off.wait()

            def strip_pass(r, carry):
                rows = rows_of(r, B)
                spot = pl.ds(pl.multiple_of(t * size + r * B, B), B)
                total = jnp.zeros((B, B), F32)
                if k == 0:
                    live_down = down(stored_row[:, spot])
                    for c in range(strips):
                        block = home[t, rows, c * B:(c + 1) * B]
                        keep = line + (r * B + shift) <= lane + c * B
                        block = jnp.where(keep, block, 0.0) * live_down * stored_col[:, t * size + c * B:t * size + (c + 1) * B]
                        home[t, rows, c * B:(c + 1) * B] = block
                        col_acc[t, :, c * B:(c + 1) * B] += folded(block)
                        total = total + block
                    corner = home[t, rows, rows]
                    diag_vec[:, spot] = jnp.where(on_diag, jnp.sum(jnp.where(line == lane, corner, 0.0), axis=0, keepdims=True), 0.0)
                else:
                    u_down = down(su[:, spot])
                    for c in range(strips):
                        block = home[t, rows, c * B:(c + 1) * B]
                        col_acc[t, :, c * B:(c + 1) * B] += folded(block * u_down)
                        total = total + block * sv[:, t * size + c * B:t * size + (c + 1) * B]
                row[:, spot] = jnp.sum(total.T, axis=0, keepdims=True)
                return carry

            lax.fori_loop(0, strips, strip_pass, 0)

        cols = jnp.concatenate([jnp.sum(col_acc[t], axis=0, keepdims=True) for t in range(2)], axis=1) * sv[...]
        rows2 = put_home(row[...] * su[...])
        corner2 = put_home(diag_vec[...] * su[...] * sv[...])
        cols2 = put_home(cols)
        zero = jnp.zeros((2, size), F32)
        mine = rows2 + jnp.where(on_diag, cols2 - corner2, jnp.concatenate([zero, cols2[:, :size]], axis=1))
        edge = jnp.where(on_diag, 0.0, cols2[:, size:])
        if k > 0:
            mean = settle(k - 1)
            mine, edge = (jnp.where(value != 0, value * mean * mean, 0.0) for value in (mine, edge))
        quad[k, slot] = mine
        edge_out[k] = edge
        partial = jnp.sum(mine) + jnp.sum(edge)
        kept = jnp.where(on_diag, jnp.sum(mask[...].astype(F32)), 0.0)
        marked = jnp.full((1, B), placed[1]).astype(F32)
        tot[k, me] = jnp.where(first_lane == 0, partial, jnp.where(first_lane == 1, kept, jnp.where(first_lane == 2, marked, 0.0)))

        def quad_copy(off):
            q = lax.rem(slot + off, 4)
            return remote(quad.at[k, slot], quad.at[k, slot], quad_sem.at[k, 0], quad_sem.at[k, 1], (spot_l + (q // 2) * half, lax.rem(q, 2)))

        nxt_copies = [remote(quad.at[k, slot, :, :size], nxt.at[k, slot], nxt_sem.at[k, 0], nxt_sem.at[k, 1], (prev_l + i * half, 1)) for i in range(2)]
        edge_copies = [remote(edge_out.at[k], edge_in.at[k, side], edge_sem.at[k, 0], edge_sem.at[k, 1], (next_l + (i // 2) * half, i % 2)) for i in range(4)]
        epair = remote(edge_out.at[k], edge_pair.at[k], epair_sem.at[k, 0], epair_sem.at[k, 1], partner)

        for off in range(1, 4):
            quad_copy(off).start()
        for copy in nxt_copies:
            copy.start()

        @pl.when(off_diag)
        def _():
            for copy in edge_copies:
                copy.start()
            epair.start()

        def tot_start(off, carry):
            remote(tot.at[k, me], tot.at[k, me], tot_sem.at[k, 0], tot_sem.at[k, 1], other(off)).start()
            return carry

        lax.fori_loop(1, count, tot_start, 0)

        if k == 0:
            for off in range(1, group):
                start_scatter(off)
            start_bulk(1)
        else:
            start_bulk(2)

        def wait_all(ref, sem):
            pltpu.make_async_copy(ref, ref, sem).wait()

        wait_all(quad.at[k, pl.ds(0, 3)], quad_sem.at[k, 1])
        wait_all(edge_in.at[k], edge_sem.at[k, 1])

        @pl.when(off_diag)
        def _():
            wait_all(nxt.at[k], nxt_sem.at[k, 1])
            epair.wait_recv()

        wait_all(quad.at[k, pl.ds(0, 3)], quad_sem.at[k, 0])
        wait_all(nxt.at[k, pl.ds(0, 2)], nxt_sem.at[k, 0])

        @pl.when(off_diag)
        def _():
            wait_all(edge_in.at[k], edge_sem.at[k, 0])
            wait_all(edge_in.at[k], edge_sem.at[k, 0])
            epair.wait_send()

        sums = (quad[k, 0] + quad[k, 1]) + (quad[k, 2] + quad[k, 3])
        arrived = from_prev(edge_in[k, 0] + edge_in[k, 1])
        sums = sums + jnp.concatenate([arrived, jnp.zeros((2, size), F32)], axis=1)
        sums_now[...] = own_of(sums)
        inverse = 1.0 / jnp.where(live2[...] > 0, sums, 1.0)
        u2[...] = u2[...] * inverse

        @pl.when(on_diag)
        def _():
            v2[...] = v2[...] * inverse

        @pl.when(off_diag)
        def _():
            next_sums = from_next((nxt[k, 0] + nxt[k, 1]) + (nxt[k, 2] + nxt[k, 3])) + (edge_out[k] + edge_pair[k])
            next_inverse = 1.0 / jnp.where(nlive2[...] > 0, next_sums, 1.0)
            v2[...] = v2[...] * jnp.concatenate([inverse[:, size:], next_inverse], axis=1)

        su[...] = stored(u2[...])
        sv[...] = stored(v2[...])

    settle(ITERS - 1)
    u_out[...] = own_of(jnp.where(live2[...] > 0, u2[...], 0.0))
    v_out[...] = own_of(jnp.where(live_col2[...] > 0, v2[...], 0.0))

    best = None
    for g in range(half // group):
        several = tot[0, g * group * 2]
        for p in range(1, group):
            several = several + tot[0, (g * group + p) * 2]
        best = several if best is None else jnp.maximum(best, several)
    flags_out[group] = jnp.sum(jnp.where(first_lane == 2, best, 0.0)).astype(jnp.int32)
    for p in range(group):
        flags_out[p] = jnp.sum(jnp.where(first_lane == 2, tot[0, (base_chip + p) * 2], 0.0)).astype(jnp.int32)

    diag_out[...] = jnp.zeros_like(diag_out)

    @pl.when(on_diag)
    def _():
        raw_send.wait()
        diag_out[...] = jnp.where(gone == 1, raw_in[...], raw_vec[...])
        own_diag.wait()
        for i in range(2):
            wait_pair = pltpu.make_async_copy(arr0.at[:, :part], arr0.at[:, :part], bulk_sem.at[i])
            wait_pair.wait()
            others = pieces.at[pl.ds(0, group - 1), :part]
            pltpu.make_async_copy(others, others, scat_sem.at[i]).wait()

    @pl.when(off_diag)
    def _():
        for i in range(2):
            sent = arr0.at[pl.ds(0, early_of(size))]
            pltpu.make_async_copy(sent, sent, bulk_sem.at[i]).wait()
            others = pieces.at[pl.ds(0, group - 1)]
            pltpu.make_async_copy(others, others, scat_sem.at[i]).wait()


def second(n, size, k, flags, pieces, held, arr1, rest, *scratch):
    pin, stage, outb = scratch[:3]
    slots = scratch[3:3 + SUBS]
    in_sem, mid_sem, dist_sem, own_sem, rest_sem = scratch[3 + SUBS:]
    b, d = lax.axis_index("bins"), lax.axis_index("diag")
    half, group = n // 2, size // B
    strips = size // B
    on_diag, off_diag = d == 0, d == 1
    partner = (lax.rem(b + half, n), d)
    place_in = lax.rem(b, group)
    base_chip = b - place_in

    def mate(off):
        return (base_chip + flip(place_in, off), d)

    def send_rest(first, last):
        for r in range(first, last):
            pltpu.make_async_remote_copy(
                held.at[0, 0, pl.ds(r * B, B)], rest.at[r - early_of(size)], rest_sem.at[0], rest_sem.at[1], device_id=partner, device_id_type=MESH).start()

    def run(tall, has_rest):
        sub = tall // SUBS
        if k > 0:
            load = pltpu.make_async_copy(pieces.at[:, :tall], pin.at[:, :tall], in_sem.at[0])
            load.start()
        barrier = pltpu.get_barrier_semaphore()
        pl.semaphore_signal(barrier, inc=1, device_id=partner, device_id_type=MESH)
        for off in range(1, group):
            pl.semaphore_signal(barrier, inc=1, device_id=mate(off), device_id_type=MESH)

        def mid(i, s):
            return pltpu.make_async_remote_copy(
                stage.at[i, pl.ds(s * sub, sub)], slots[s].at[i, :sub], mid_sem.at[0], mid_sem.at[1 + s], device_id=partner, device_id_type=MESH)

        if k > 0:
            ranks, before = [], jnp.int32(0)
            picks = [jnp.int32(0) for _ in range(k)]
            for p in range(group):
                flag = flags[p]
                for i in range(k):
                    picks[i] = picks[i] + jnp.where(before == i, flag, 0) * p
                ranks.append(jnp.minimum(before, k - 1))
                before = before + flag
            load.wait()
            for i in range(k):
                stage[i, :tall] = pin[picks[i], :tall]
        pl.semaphore_wait(barrier, group)
        if k > 0:
            for s in range(SUBS):
                for i in range(k):
                    mid(i, s).start()
            for s in range(SUBS):
                if has_rest and s == SUBS // 2:
                    send_rest(early_of(size), early_of(size) + 1)
                rows = pl.ds(s * sub, sub)
                landed = slots[s].at[:, :sub]
                pltpu.make_async_copy(landed, landed, mid_sem.at[1 + s]).wait()
                for p in range(group):
                    outb[p, s * sub:(s + 1) * sub] = slots[s][ranks[p], :sub]
                pltpu.make_async_copy(outb.at[place_in, rows], arr1.at[place_in, rows], own_sem.at[0]).start()
                for off in range(1, group):
                    pltpu.make_async_remote_copy(
                        outb.at[flip(place_in, off), rows], arr1.at[place_in, rows], dist_sem.at[0], dist_sem.at[1],
                        device_id=mate(off), device_id_type=MESH).start()
        if has_rest:
            send_rest(early_of(size) + 1 if k > 0 else early_of(size), strips)
        if k > 0:
            sent = stage.at[:, :tall]
            pltpu.make_async_copy(sent, sent, mid_sem.at[0]).wait()
            mine = outb.at[0, :tall]
            pltpu.make_async_copy(mine, mine, own_sem.at[0]).wait()
            others = outb.at[pl.ds(0, group - 1), :tall]
            for i in range(2):
                pltpu.make_async_copy(others, others, dist_sem.at[i]).wait()
        if has_rest:
            for i in range(2):
                pltpu.make_async_copy(rest, rest, rest_sem.at[i]).wait()

    @pl.when(on_diag)
    def _():
        run(B // 2, False)

    @pl.when(off_diag)
    def _():
        run(B, True)


def scaled(size, u, v, diag, out, inb, outb, in_sem, out_sem):
    strips = size // B
    part = B // 2
    line = lax.broadcasted_iota(jnp.int32, (B, B), 0)
    lane = lax.broadcasted_iota(jnp.int32, (B, B), 1)

    def rows_of(r):
        return pl.ds(pl.multiple_of(r * B, B), B)

    def down(t, r):
        return jnp.broadcast_to(u[:, pl.ds(pl.multiple_of(t * size + r * B, B), B)], (B, B)).T

    def across(t, c):
        return v[:, t * size + c * B:t * size + (c + 1) * B]

    def write(t, r, at):
        return pltpu.make_async_copy(outb.at[at], out.at[t, 0, rows_of(r)], out_sem.at[at])

    def unfold(t, arr):
        def load(e):
            return pltpu.make_async_copy(arr.at[e, :part], inb.at[e // 2, pl.ds((e % 2) * part, part)], in_sem.at[e])

        for e in range(strips):
            load(e).start()
        for j in range(strips // 2):
            for e in (2 * j, 2 * j + 1):
                load(e).wait()
            fold = inb[j, :, :B]
            at = B
            for r in (j, strips - 1 - j):
                scale = down(t, r)
                for c in range(strips):
                    if c < r:
                        block = jnp.zeros((B, B), F32)
                    elif c == r and r == j:
                        block = jnp.where(line <= lane, fold, 0.0) * scale * across(t, c)
                    elif c == r:
                        corner = diag[:, t * size + c * B:t * size + (c + 1) * B]
                        block = jnp.where(line < lane, fold.T, jnp.where(line == lane, corner, 0.0)) * scale * across(t, c)
                    else:
                        block = inb[j, :, at:at + B] * scale * across(t, c)
                        at += B
                    outb[r, :, c * B:(c + 1) * B] = block
                write(t, r, r).start()
        for r in range(strips):
            write(t, r, r).wait()

    def straight(jobs, cut=False):
        def load(source, r, at):
            return pltpu.make_async_copy(source(r), inb.at[at], in_sem.at[at])

        for t, source, first, last, base, near in jobs:
            if near is None:
                for r in range(first, last):
                    load(source, r, base + r).start()
        for t, source, first, last, base, near in jobs:
            def step(r, carry):
                at = base + r
                if near is None:
                    load(source, r, at).wait()
                scale = down(t, r)
                for c in range(strips):
                    block = inb[at, :, c * B:(c + 1) * B] if near is None else near[r - first, :, c * B:(c + 1) * B]
                    if cut:
                        block = jnp.where(line + r * B <= lane + c * B, block, 0.0)
                    outb[at, :, c * B:(c + 1) * B] = block * scale * across(t, c)
                write(t, r, at).start()
                return carry

            lax.fori_loop(first, last, step, 0)
        for t, source, first, last, base, near in jobs:
            for r in range(first, last):
                write(t, r, base + r).wait()

    return rows_of, unfold, straight


def third(size, u, v, diag, arr0, out, *scratch):
    d = lax.axis_index("diag")
    _, unfold, straight = scaled(size, u, v, diag, out, *scratch)

    @pl.when(d == 0)
    def _():
        unfold(0, arr0)

    @pl.when(d == 1)
    def _():
        straight([(0, lambda r: arr0.at[r], 0, early_of(size), 0, None)])


def fourth(size, placed, u, v, diag, bias, arr1, rest, held, done, out, bias_out, *scratch):
    del done
    d = lax.axis_index("diag")
    strips = size // B
    bias_out[...] = bias[...]
    rows_of, unfold, straight = scaled(size, u, v, diag, out, *scratch)
    moved, stays = placed[1] == 1, placed[1] != 1
    late = (0, None, early_of(size), strips, strips - early_of(size), rest)

    @pl.when((d == 0) & moved)
    def _():
        unfold(1, arr1)

    @pl.when((d == 1) & moved)
    def _():
        straight([late, (1, lambda r: arr1.at[r], 0, strips, 0, None)])

    @pl.when((d == 0) & stays)
    def _():
        straight([(1, lambda r: held.at[1, 0, rows_of(r)], 0, strips, 0, None)], cut=True)

    @pl.when((d == 1) & stays)
    def _():
        straight([late, (1, lambda r: held.at[1, 0, rows_of(r)], 0, strips, 0, None)])


def local(n, held_tiles, placed, bin_mask, bias):
    rows_dev, size = held_tiles.shape[0], held_tiles.shape[2]
    strips, width, count = size // B, rows_dev * size, n * 2
    group = strips
    assert rows_dev == 2 and (n // 2) % group == 0
    vmem, anywhere, smem = (pl.BlockSpec(memory_space=space) for space in (pltpu.VMEM, pl.ANY, pltpu.SMEM))
    wide = jax.ShapeDtypeStruct((1, width), F32)
    store = jax.ShapeDtypeStruct((strips, B, size), F32)
    dma = pltpu.SemaphoreType.DMA
    vec, vec2 = pltpu.VMEM((1, width), F32), pltpu.VMEM((2, width), F32)
    half2 = pltpu.VMEM((2, size), F32)
    arr0, pieces, flags, u, v, bias_new, diag = pl.pallas_call(
        functools.partial(first, n, size),
        out_shape=(store, store, jax.ShapeDtypeStruct((group + 1,), jnp.int32), wide, wide, wide, wide),
        in_specs=[anywhere, smem, vmem, vmem],
        out_specs=(anywhere, anywhere, smem, vmem, vmem, vmem, vmem),
        scratch_shapes=[
            pltpu.VMEM((2, size, size), F32),
            pltpu.VMEM((2, strips // 2, B, size), F32),
            pltpu.VMEM((1, width), jnp.int32),
            pltpu.VMEM((2, 1, size), jnp.int32),
            vec2, vec2, half2, vec, vec, vec2, vec2, vec, vec, vec,
            pltpu.VMEM((2, 8, size), F32),
            vec, vec, vec,
            pltpu.VMEM((ITERS, 4, 2, width), F32),
            pltpu.VMEM((ITERS, 2, size), F32),
            pltpu.VMEM((ITERS, 2, 2, size), F32),
            pltpu.VMEM((ITERS, 2, size), F32),
            pltpu.VMEM((ITERS, 4, 2, size), F32),
            pltpu.VMEM((ITERS, count, 1, B), F32),
            vec,
            dma((2,)), dma((2,)), dma((4,)), dma((2,)), dma((2,)), dma((1,)), dma((2,)),
            dma((ITERS, 2)), dma((ITERS, 2)), dma((ITERS, 2)), dma((ITERS, 2)), dma((ITERS, 2)),
        ],
        compiler_params=pltpu.CompilerParams(collective_id=0, has_side_effects=True),
    )(held_tiles, placed, bin_mask.reshape(1, width), bias.reshape(1, width))

    left = strips - early_of(size)
    remain = jax.ShapeDtypeStruct((left, B, size), F32)

    def branch(k):
        sub, most = B // SUBS, max(k, 1)
        return lambda flags, pieces, held: pl.pallas_call(
            functools.partial(second, n, size, k),
            out_shape=(store, remain),
            in_specs=[smem, anywhere, anywhere],
            out_specs=(anywhere, anywhere),
            scratch_shapes=[
                pltpu.VMEM((strips, B, size), F32),
                pltpu.VMEM((most, B, size), F32),
                pltpu.VMEM((strips, B, size), F32),
                *[pltpu.VMEM((most, sub, size), F32) for _ in range(SUBS)],
                dma((1,)), dma((1 + SUBS,)), dma((2,)), dma((1,)), dma((2,)),
            ],
            compiler_params=pltpu.CompilerParams(collective_id=1 + k, has_side_effects=True, vmem_limit_bytes=GRANT),
        )(flags, pieces, held)

    whole = jax.ShapeDtypeStruct((rows_dev, 1, size, size), F32)

    def strip_scratch(slots):
        return [pltpu.VMEM((slots, B, size), F32), pltpu.VMEM((slots, B, size), F32), dma((slots,)), dma((slots,))]

    balanced = pl.pallas_call(
        functools.partial(third, size),
        out_shape=whole,
        in_specs=[vmem, vmem, vmem, anywhere],
        out_specs=anywhere,
        scratch_shapes=strip_scratch(strips),
    )(u, v, diag, arr0)
    flags, balanced = lax.optimization_barrier((flags, balanced))
    arr1, rest = lax.switch(flags[group], [branch(k) for k in range(group + 1)], flags, pieces, held_tiles)
    balanced, bias_new = pl.pallas_call(
        functools.partial(fourth, size),
        out_shape=(whole, wide),
        in_specs=[smem, vmem, vmem, vmem, vmem, anywhere, vmem, anywhere, anywhere],
        out_specs=(anywhere, vmem),
        scratch_shapes=strip_scratch(strips + left),
        input_output_aliases={8: 0},
        compiler_params=pltpu.CompilerParams(vmem_limit_bytes=GRANT),
    )(placed, u, v, diag, bias_new, arr1, rest, held_tiles, balanced)
    return balanced, bias_new.reshape(width)


def solution(mesh):
    specs = (P("bins", "diag", None, None), P("bins"), P("bins"), P("bins"))
    return jax.shard_map(
        functools.partial(local, mesh.shape["bins"]),
        mesh=mesh,
        in_specs=specs,
        out_specs=(P("bins", "diag", None, None), P("bins")),
        check_vma=False,
    )
```

```python
import functools

import jax
import jax.numpy as jnp
from jax import lax
from jax.experimental import pallas as pl
from jax.experimental.pallas import tpu as pltpu
from jax.sharding import PartitionSpec as P

ITERS = 2
B = 128
SUBS = 8
GRANT = 52 << 20
MESH = pl.DeviceIdType.MESH
F32 = jnp.float32


def early_of(size):
    return size // B // 2


def flip(place, mask):
    out, bit = 0, 1
    while bit <= mask:
        digit = lax.rem(place // bit, 2)
        out = out + bit * (1 - digit if mask & bit else digit)
        bit *= 2
    return out + place // bit * bit


def first(n, size, held, placed, mask, bias, arr0, pieces, flags_out, u_out, v_out, bias_out, diag_out,
          home, pack, p_mask, next_mask, live2, live_col2, nlive2, stored_row, stored_col, u2, v2, su, sv, row, col_acc, diag_vec, raw_vec, raw_in,
          quad, edge_out, edge_in, edge_pair, nxt, tot, sums_now,
          in_sem, mask_sem, nmask_sem, bulk_sem, scat_sem, own_sem, raw_sem, quad_sem, edge_sem, epair_sem, nxt_sem, tot_sem):
    b, d = lax.axis_index("bins"), lax.axis_index("diag")
    half = n // 2
    count = n * 2
    me = b * 2 + d
    on_diag, off_diag = d == 0, d == 1
    strips = size // B
    group = strips
    width = 2 * size
    part = B // 2
    side = b // half
    spot_l = lax.rem(b, half)
    partner = (lax.rem(b + half, n), d)
    slot = side * 2 + d
    prev_l, next_l = lax.rem(spot_l + half - 1, half), lax.rem(spot_l + 1, half)
    place_in = lax.rem(b, group)
    base_chip = b - place_in

    def remote(src, dst, send, recv, device):
        return pltpu.make_async_remote_copy(src, dst, send, recv, device_id=device, device_id_type=MESH)

    def other(off):
        target = lax.rem(me + off, count)
        return (target // 2, lax.rem(target, 2))

    barrier = pltpu.get_barrier_semaphore()

    for off in range(1, count):
        pl.semaphore_signal(barrier, inc=1, device_id=other(off), device_id_type=MESH)
    loads = []
    for t in range(2):
        loads.append(pltpu.make_async_copy(held.at[t, 0], home.at[t], in_sem.at[t]))
        loads[-1].start()
    pl.semaphore_wait(barrier, count - 1)

    mask_send = remote(mask, p_mask, mask_sem.at[0], mask_sem.at[1], partner)
    mask_send.start()
    nmask = [remote(mask.at[:, :size], next_mask.at[side], nmask_sem.at[i], nmask_sem.at[2 + side], (prev_l + i * half, 1)) for i in range(2)]

    @pl.when(on_diag)
    def _():
        for copy in nmask:
            copy.start()

    def rows_of(e, tall):
        return pl.ds(pl.multiple_of(e * tall, tall), tall)

    def bulk(e):
        diag_part = remote(pack.at[0, e // 2, pl.ds((e % 2) * part, part)], arr0.at[e, :part], bulk_sem.at[0], bulk_sem.at[1], partner)
        off_part = remote(held.at[0, 0, pl.ds(e * B, B)], arr0.at[e], bulk_sem.at[0], bulk_sem.at[1], partner)
        return diag_part, off_part

    def start_bulk(stage):
        @pl.when(on_diag)
        def _():
            for e in diag_cuts[stage]:
                bulk(e)[0].start()

        @pl.when(off_diag)
        def _():
            for e in off_cuts[stage]:
                bulk(e)[1].start()

    def start_scatter(off):
        e = flip(place_in, off)

        @pl.when(on_diag)
        def _():
            remote(pack.at[1, e // 2, rows_of(lax.rem(e, 2), part)], pieces.at[place_in, :part], scat_sem.at[0], scat_sem.at[1], (base_chip + e, d)).start()

        @pl.when(off_diag)
        def _():
            remote(held.at[1, 0, rows_of(e, B)], pieces.at[place_in], scat_sem.at[0], scat_sem.at[1], (base_chip + e, d)).start()

    line = lax.broadcasted_iota(jnp.int32, (B, B), 0)
    lane = lax.broadcasted_iota(jnp.int32, (B, B), 1)

    def fold_tile(t):
        for j in range(strips // 2):
            k = strips - 1 - j
            low, high = home[t, j * B:(j + 1) * B, j * B:(j + 1) * B], home[t, k * B:(k + 1) * B, k * B:(k + 1) * B]
            pack[t, j, :, :B] = jnp.where(line <= lane, low, high.T)
            mid = (strips - j) * B
            pack[t, j, :, B:mid] = home[t, j * B:(j + 1) * B, (j + 1) * B:]
            if mid < size:
                pack[t, j, :, mid:] = home[t, k * B:(k + 1) * B, (k + 1) * B:]

            for q, block in ((j, low), (k, high)):
                raw_vec[:, t * size + q * B:t * size + (q + 1) * B] = jnp.sum(jnp.where(line == lane, block, 0.0), axis=0, keepdims=True)

    own_off = pltpu.make_async_copy(home.at[1, rows_of(place_in, B)], pieces.at[place_in], own_sem.at[0])
    own_diag = pltpu.make_async_copy(pack.at[1, place_in // 2, rows_of(lax.rem(place_in, 2), part)], pieces.at[place_in, :part], own_sem.at[0])
    raw_send = remote(raw_vec, raw_in, raw_sem.at[0], raw_sem.at[1], partner)

    diag_cuts = (range(0), range(1), range(1, strips))
    off_cuts = (range(early_of(size) - 2), range(early_of(size) - 2, early_of(size) - 1), range(early_of(size) - 1, early_of(size)))

    @pl.when(off_diag)
    def _():
        for e in off_cuts[0]:
            bulk(e)[1].start()

    for t in range(2):
        loads[t].wait()

    @pl.when(on_diag)
    def _():
        fold_tile(0)
        for e in diag_cuts[0]:
            bulk(e)[0].start()
        fold_tile(1)
        own_diag.start()
        raw_send.start()

    @pl.when(off_diag)
    def _():
        own_off.start()

    mask_send.wait()

    @pl.when(off_diag)
    def _():
        for i in range(2):
            remote(mask.at[:, :size], next_mask.at[i], nmask_sem.at[0], nmask_sem.at[2 + i], partner).wait_recv()

    @pl.when(on_diag)
    def _():
        for copy in nmask:
            copy.wait_send()

    def pair_of(own, their):
        lower, upper = jnp.where(side == 0, own, their), jnp.where(side == 0, their, own)
        return jnp.concatenate([lower, upper], axis=0)

    def own_of(both):
        return jnp.where(side == 0, both[0:1], both[1:2])

    flag = jnp.full((1, size), placed[1]) == 1
    gone = jnp.concatenate([jnp.ones((1, size), jnp.int32), flag.astype(jnp.int32)], axis=1)
    at_side = jnp.where(gone == 1, 1 - side, side)

    def stored(both):
        return jnp.where(at_side == 0, both[0:1], both[1:2])

    sides = lax.broadcasted_iota(jnp.int32, (2, width), 0)

    def put_home(vector):
        return jnp.where(sides == at_side, vector, 0.0)

    def from_next(both):
        return jnp.where(spot_l == half - 1, jnp.concatenate([both[1:2], jnp.zeros_like(both[0:1])], axis=0), both)

    def from_prev(both):
        return jnp.where(spot_l == 0, jnp.concatenate([jnp.zeros_like(both[0:1]), both[0:1]], axis=0), both)

    live2[...] = pair_of(mask[...].astype(F32), p_mask[...].astype(F32))
    nlive2[...] = jnp.zeros_like(nlive2)

    @pl.when(off_diag)
    def _():
        nlive2[...] = from_next(jnp.concatenate([next_mask[0], next_mask[1]], axis=0).astype(F32))

    live_col2[...] = jnp.where(on_diag, live2[...], jnp.concatenate([live2[:, size:], nlive2[...]], axis=1))
    stored_row[...] = stored(live2[...])
    stored_col[...] = stored(live_col2[...])
    u2[...] = jnp.ones_like(u2)
    v2[...] = jnp.ones_like(v2)
    su[...] = jnp.ones_like(su)
    sv[...] = jnp.ones_like(sv)
    bias_out[...] = bias[...]
    shift = jnp.where(on_diag, 0, -2 * size)

    def down(vector):
        return jnp.broadcast_to(vector, (B, B)).T

    def folded(block):
        return jnp.sum(block.reshape(B // 8, 8, B), axis=0)

    first_lane = lax.broadcasted_iota(jnp.int32, (1, B), 1)

    def settle(k):
        many = tot.at[k, pl.ds(0, count - 1)]
        pltpu.make_async_copy(many, many, tot_sem.at[k, 0]).wait()
        pltpu.make_async_copy(many, many, tot_sem.at[k, 1]).wait()
        both = jnp.sum(tot[k], axis=0)
        mean = jnp.sum(jnp.where(first_lane == 0, both, 0.0), axis=1, keepdims=True) / jnp.sum(
            jnp.where(first_lane == 1, both, 0.0), axis=1, keepdims=True)
        bias_out[...] = bias_out[...] * jnp.where(mask[...] > 0, sums_now[...] / mean, 1.0)
        u2[...] = u2[...] * jnp.where(live2[...] > 0, mean, 1.0)
        v2[...] = v2[...] * jnp.where(live_col2[...] > 0, mean, 1.0)
        return mean

    for k in range(ITERS):
        col_acc[...] = jnp.zeros_like(col_acc)
        for t in range(2):
            if k == 0 and t == 1:
                @pl.when(off_diag)
                def _():
                    own_off.wait()

            def strip_pass(r, carry):
                rows = rows_of(r, B)
                spot = pl.ds(pl.multiple_of(t * size + r * B, B), B)
                total = jnp.zeros((B, B), F32)
                if k == 0:
                    live_down = down(stored_row[:, spot])
                    for c in range(strips):
                        block = home[t, rows, c * B:(c + 1) * B]
                        keep = line + (r * B + shift) <= lane + c * B
                        block = jnp.where(keep, block, 0.0) * live_down * stored_col[:, t * size + c * B:t * size + (c + 1) * B]
                        home[t, rows, c * B:(c + 1) * B] = block
                        col_acc[t, :, c * B:(c + 1) * B] += folded(block)
                        total = total + block
                    corner = home[t, rows, rows]
                    diag_vec[:, spot] = jnp.where(on_diag, jnp.sum(jnp.where(line == lane, corner, 0.0), axis=0, keepdims=True), 0.0)
                else:
                    u_down = down(su[:, spot])
                    for c in range(strips):
                        block = home[t, rows, c * B:(c + 1) * B]
                        col_acc[t, :, c * B:(c + 1) * B] += folded(block * u_down)
                        total = total + block * sv[:, t * size + c * B:t * size + (c + 1) * B]
                row[:, spot] = jnp.sum(total.T, axis=0, keepdims=True)
                return carry

            lax.fori_loop(0, strips, strip_pass, 0)

        cols = jnp.concatenate([jnp.sum(col_acc[t], axis=0, keepdims=True) for t in range(2)], axis=1) * sv[...]
        rows2 = put_home(row[...] * su[...])
        corner2 = put_home(diag_vec[...] * su[...] * sv[...])
        cols2 = put_home(cols)
        zero = jnp.zeros((2, size), F32)
        mine = rows2 + jnp.where(on_diag, cols2 - corner2, jnp.concatenate([zero, cols2[:, :size]], axis=1))
        edge = jnp.where(on_diag, 0.0, cols2[:, size:])
        if k > 0:
            mean = settle(k - 1)
            mine, edge = (jnp.where(value != 0, value * mean * mean, 0.0) for value in (mine, edge))
        quad[k, slot] = mine
        edge_out[k] = edge
        partial = jnp.sum(mine) + jnp.sum(edge)
        kept = jnp.where(on_diag, jnp.sum(mask[...].astype(F32)), 0.0)
        marked = jnp.full((1, B), placed[1]).astype(F32)
        tot[k, me] = jnp.where(first_lane == 0, partial, jnp.where(first_lane == 1, kept, jnp.where(first_lane == 2, marked, 0.0)))

        def quad_copy(off):
            q = lax.rem(slot + off, 4)
            return remote(quad.at[k, slot], quad.at[k, slot], quad_sem.at[k, 0], quad_sem.at[k, 1], (spot_l + (q // 2) * half, lax.rem(q, 2)))

        nxt_copies = [remote(quad.at[k, slot, :, :size], nxt.at[k, slot], nxt_sem.at[k, 0], nxt_sem.at[k, 1], (prev_l + i * half, 1)) for i in range(2)]
        edge_copies = [remote(edge_out.at[k], edge_in.at[k, side], edge_sem.at[k, 0], edge_sem.at[k, 1], (next_l + (i // 2) * half, i % 2)) for i in range(4)]
        epair = remote(edge_out.at[k], edge_pair.at[k], epair_sem.at[k, 0], epair_sem.at[k, 1], partner)

        for off in range(1, 4):
            quad_copy(off).start()
        for copy in nxt_copies:
            copy.start()

        @pl.when(off_diag)
        def _():
            for copy in edge_copies:
                copy.start()
            epair.start()

        def tot_start(off, carry):
            remote(tot.at[k, me], tot.at[k, me], tot_sem.at[k, 0], tot_sem.at[k, 1], other(off)).start()
            return carry

        lax.fori_loop(1, count, tot_start, 0)

        if k == 0:
            for off in range(1, group):
                start_scatter(off)
            start_bulk(1)
        else:
            start_bulk(2)

        def wait_all(ref, sem):
            pltpu.make_async_copy(ref, ref, sem).wait()

        wait_all(quad.at[k, pl.ds(0, 3)], quad_sem.at[k, 1])
        wait_all(edge_in.at[k], edge_sem.at[k, 1])

        @pl.when(off_diag)
        def _():
            wait_all(nxt.at[k], nxt_sem.at[k, 1])
            epair.wait_recv()

        wait_all(quad.at[k, pl.ds(0, 3)], quad_sem.at[k, 0])
        wait_all(nxt.at[k, pl.ds(0, 2)], nxt_sem.at[k, 0])

        @pl.when(off_diag)
        def _():
            wait_all(edge_in.at[k], edge_sem.at[k, 0])
            wait_all(edge_in.at[k], edge_sem.at[k, 0])
            epair.wait_send()

        sums = (quad[k, 0] + quad[k, 1]) + (quad[k, 2] + quad[k, 3])
        arrived = from_prev(edge_in[k, 0] + edge_in[k, 1])
        sums = sums + jnp.concatenate([arrived, jnp.zeros((2, size), F32)], axis=1)
        sums_now[...] = own_of(sums)
        inverse = 1.0 / jnp.where(live2[...] > 0, sums, 1.0)
        u2[...] = u2[...] * inverse

        @pl.when(on_diag)
        def _():
            v2[...] = v2[...] * inverse

        @pl.when(off_diag)
        def _():
            next_sums = from_next((nxt[k, 0] + nxt[k, 1]) + (nxt[k, 2] + nxt[k, 3])) + (edge_out[k] + edge_pair[k])
            next_inverse = 1.0 / jnp.where(nlive2[...] > 0, next_sums, 1.0)
            v2[...] = v2[...] * jnp.concatenate([inverse[:, size:], next_inverse], axis=1)

        su[...] = stored(u2[...])
        sv[...] = stored(v2[...])

    settle(ITERS - 1)
    u_out[...] = own_of(jnp.where(live2[...] > 0, u2[...], 0.0))
    v_out[...] = own_of(jnp.where(live_col2[...] > 0, v2[...], 0.0))

    best = None
    for g in range(half // group):
        several = tot[0, g * group * 2]
        for p in range(1, group):
            several = several + tot[0, (g * group + p) * 2]
        best = several if best is None else jnp.maximum(best, several)
    flags_out[group] = jnp.sum(jnp.where(first_lane == 2, best, 0.0)).astype(jnp.int32)
    for p in range(group):
        flags_out[p] = jnp.sum(jnp.where(first_lane == 2, tot[0, (base_chip + p) * 2], 0.0)).astype(jnp.int32)

    diag_out[...] = jnp.zeros_like(diag_out)

    @pl.when(on_diag)
    def _():
        raw_send.wait()
        diag_out[...] = jnp.where(gone == 1, raw_in[...], raw_vec[...])
        own_diag.wait()
        for i in range(2):
            wait_pair = pltpu.make_async_copy(arr0.at[:, :part], arr0.at[:, :part], bulk_sem.at[i])
            wait_pair.wait()
            others = pieces.at[pl.ds(0, group - 1), :part]
            pltpu.make_async_copy(others, others, scat_sem.at[i]).wait()

    @pl.when(off_diag)
    def _():
        for i in range(2):
            sent = arr0.at[pl.ds(0, early_of(size))]
            pltpu.make_async_copy(sent, sent, bulk_sem.at[i]).wait()
            others = pieces.at[pl.ds(0, group - 1)]
            pltpu.make_async_copy(others, others, scat_sem.at[i]).wait()


def second(n, size, k, flags, pieces, held, arr1, rest, *scratch):
    pin, stage, outb = scratch[:3]
    slots = scratch[3:3 + SUBS]
    in_sem, mid_sem, dist_sem, own_sem, rest_sem = scratch[3 + SUBS:]
    b, d = lax.axis_index("bins"), lax.axis_index("diag")
    half, group = n // 2, size // B
    strips = size // B
    on_diag, off_diag = d == 0, d == 1
    partner = (lax.rem(b + half, n), d)
    place_in = lax.rem(b, group)
    base_chip = b - place_in

    def mate(off):
        return (base_chip + flip(place_in, off), d)

    def send_rest(first, last):
        for r in range(first, last):
            pltpu.make_async_remote_copy(
                held.at[0, 0, pl.ds(r * B, B)], rest.at[r - early_of(size)], rest_sem.at[0], rest_sem.at[1], device_id=partner, device_id_type=MESH).start()

    def run(tall, has_rest):
        sub = tall // SUBS
        if k > 0:
            load = pltpu.make_async_copy(pieces.at[:, :tall], pin.at[:, :tall], in_sem.at[0])
            load.start()
        barrier = pltpu.get_barrier_semaphore()
        pl.semaphore_signal(barrier, inc=1, device_id=partner, device_id_type=MESH)
        for off in range(1, group):
            pl.semaphore_signal(barrier, inc=1, device_id=mate(off), device_id_type=MESH)

        def mid(i, s):
            return pltpu.make_async_remote_copy(
                stage.at[i, pl.ds(s * sub, sub)], slots[s].at[i, :sub], mid_sem.at[0], mid_sem.at[1 + s], device_id=partner, device_id_type=MESH)

        if k > 0:
            ranks, before = [], jnp.int32(0)
            picks = [jnp.int32(0) for _ in range(k)]
            for p in range(group):
                flag = flags[p]
                for i in range(k):
                    picks[i] = picks[i] + jnp.where(before == i, flag, 0) * p
                ranks.append(jnp.minimum(before, k - 1))
                before = before + flag
            load.wait()
            for i in range(k):
                stage[i, :tall] = pin[picks[i], :tall]
        pl.semaphore_wait(barrier, group)
        if k > 0:
            for s in range(SUBS):
                for i in range(k):
                    mid(i, s).start()
            for s in range(SUBS):
                if has_rest and s == SUBS // 2:
                    send_rest(early_of(size), early_of(size) + 1)
                rows = pl.ds(s * sub, sub)
                landed = slots[s].at[:, :sub]
                pltpu.make_async_copy(landed, landed, mid_sem.at[1 + s]).wait()
                for p in range(group):
                    outb[p, s * sub:(s + 1) * sub] = slots[s][ranks[p], :sub]
                pltpu.make_async_copy(outb.at[place_in, rows], arr1.at[place_in, rows], own_sem.at[0]).start()
                for off in range(1, group):
                    pltpu.make_async_remote_copy(
                        outb.at[flip(place_in, off), rows], arr1.at[place_in, rows], dist_sem.at[0], dist_sem.at[1],
                        device_id=mate(off), device_id_type=MESH).start()
        if has_rest:
            send_rest(early_of(size) + 1 if k > 0 else early_of(size), strips)
        if k > 0:
            sent = stage.at[:, :tall]
            pltpu.make_async_copy(sent, sent, mid_sem.at[0]).wait()
            mine = outb.at[0, :tall]
            pltpu.make_async_copy(mine, mine, own_sem.at[0]).wait()
            others = outb.at[pl.ds(0, group - 1), :tall]
            for i in range(2):
                pltpu.make_async_copy(others, others, dist_sem.at[i]).wait()
        if has_rest:
            for i in range(2):
                pltpu.make_async_copy(rest, rest, rest_sem.at[i]).wait()

    @pl.when(on_diag)
    def _():
        run(B // 2, False)

    @pl.when(off_diag)
    def _():
        run(B, True)


def scaled(size, u, v, diag, out, inb, outb, in_sem, out_sem):
    strips = size // B
    part = B // 2
    line = lax.broadcasted_iota(jnp.int32, (B, B), 0)
    lane = lax.broadcasted_iota(jnp.int32, (B, B), 1)

    def rows_of(r):
        return pl.ds(pl.multiple_of(r * B, B), B)

    def down(t, r):
        return jnp.broadcast_to(u[:, pl.ds(pl.multiple_of(t * size + r * B, B), B)], (B, B)).T

    def across(t, c):
        return v[:, t * size + c * B:t * size + (c + 1) * B]

    def write(t, r, at):
        return pltpu.make_async_copy(outb.at[at], out.at[t, 0, rows_of(r)], out_sem.at[at])

    def unfold(t, arr):
        def load(e):
            return pltpu.make_async_copy(arr.at[e, :part], inb.at[e // 2, pl.ds((e % 2) * part, part)], in_sem.at[e])

        for e in range(strips):
            load(e).start()
        for j in range(strips // 2):
            for e in (2 * j, 2 * j + 1):
                load(e).wait()
            fold = inb[j, :, :B]
            at = B
            for r in (j, strips - 1 - j):
                scale = down(t, r)
                for c in range(strips):
                    if c < r:
                        block = jnp.zeros((B, B), F32)
                    elif c == r and r == j:
                        block = jnp.where(line <= lane, fold, 0.0) * scale * across(t, c)
                    elif c == r:
                        corner = diag[:, t * size + c * B:t * size + (c + 1) * B]
                        block = jnp.where(line < lane, fold.T, jnp.where(line == lane, corner, 0.0)) * scale * across(t, c)
                    else:
                        block = inb[j, :, at:at + B] * scale * across(t, c)
                        at += B
                    outb[r, :, c * B:(c + 1) * B] = block
                write(t, r, r).start()
        for r in range(strips):
            write(t, r, r).wait()

    def straight(jobs, cut=False):
        def load(source, r, at):
            return pltpu.make_async_copy(source(r), inb.at[at], in_sem.at[at])

        for t, source, first, last, base, near in jobs:
            if near is None:
                for r in range(first, last):
                    load(source, r, base + r).start()
        for t, source, first, last, base, near in jobs:
            def step(r, carry):
                at = base + r
                if near is None:
                    load(source, r, at).wait()
                scale = down(t, r)
                for c in range(strips):
                    block = inb[at, :, c * B:(c + 1) * B] if near is None else near[r - first, :, c * B:(c + 1) * B]
                    if cut:
                        block = jnp.where(line + r * B <= lane + c * B, block, 0.0)
                    outb[at, :, c * B:(c + 1) * B] = block * scale * across(t, c)
                write(t, r, at).start()
                return carry

            lax.fori_loop(first, last, step, 0)
        for t, source, first, last, base, near in jobs:
            for r in range(first, last):
                write(t, r, base + r).wait()

    return rows_of, unfold, straight


def third(size, u, v, diag, arr0, out, *scratch):
    d = lax.axis_index("diag")
    _, unfold, straight = scaled(size, u, v, diag, out, *scratch)

    @pl.when(d == 0)
    def _():
        unfold(0, arr0)

    @pl.when(d == 1)
    def _():
        straight([(0, lambda r: arr0.at[r], 0, early_of(size), 0, None)])


def fourth(size, placed, u, v, diag, bias, arr1, rest, held, done, out, bias_out, *scratch):
    del done
    d = lax.axis_index("diag")
    strips = size // B
    bias_out[...] = bias[...]
    rows_of, unfold, straight = scaled(size, u, v, diag, out, *scratch)
    moved, stays = placed[1] == 1, placed[1] != 1
    late = (0, None, early_of(size), strips, strips - early_of(size), rest)

    @pl.when((d == 0) & moved)
    def _():
        unfold(1, arr1)

    @pl.when((d == 1) & moved)
    def _():
        straight([late, (1, lambda r: arr1.at[r], 0, strips, 0, None)])

    @pl.when((d == 0) & stays)
    def _():
        straight([(1, lambda r: held.at[1, 0, rows_of(r)], 0, strips, 0, None)], cut=True)

    @pl.when((d == 1) & stays)
    def _():
        straight([late, (1, lambda r: held.at[1, 0, rows_of(r)], 0, strips, 0, None)])


def local(n, held_tiles, placed, bin_mask, bias):
    rows_dev, size = held_tiles.shape[0], held_tiles.shape[2]
    strips, width, count = size // B, rows_dev * size, n * 2
    group = strips
    assert rows_dev == 2 and (n // 2) % group == 0
    vmem, anywhere, smem = (pl.BlockSpec(memory_space=space) for space in (pltpu.VMEM, pl.ANY, pltpu.SMEM))
    wide = jax.ShapeDtypeStruct((1, width), F32)
    store = jax.ShapeDtypeStruct((strips, B, size), F32)
    dma = pltpu.SemaphoreType.DMA
    vec, vec2 = pltpu.VMEM((1, width), F32), pltpu.VMEM((2, width), F32)
    half2 = pltpu.VMEM((2, size), F32)
    arr0, pieces, flags, u, v, bias_new, diag = pl.pallas_call(
        functools.partial(first, n, size),
        out_shape=(store, store, jax.ShapeDtypeStruct((group + 1,), jnp.int32), wide, wide, wide, wide),
        in_specs=[anywhere, smem, vmem, vmem],
        out_specs=(anywhere, anywhere, smem, vmem, vmem, vmem, vmem),
        scratch_shapes=[
            pltpu.VMEM((2, size, size), F32),
            pltpu.VMEM((2, strips // 2, B, size), F32),
            pltpu.VMEM((1, width), jnp.int32),
            pltpu.VMEM((2, 1, size), jnp.int32),
            vec2, vec2, half2, vec, vec, vec2, vec2, vec, vec, vec,
            pltpu.VMEM((2, 8, size), F32),
            vec, vec, vec,
            pltpu.VMEM((ITERS, 4, 2, width), F32),
            pltpu.VMEM((ITERS, 2, size), F32),
            pltpu.VMEM((ITERS, 2, 2, size), F32),
            pltpu.VMEM((ITERS, 2, size), F32),
            pltpu.VMEM((ITERS, 4, 2, size), F32),
            pltpu.VMEM((ITERS, count, 1, B), F32),
            vec,
            dma((2,)), dma((2,)), dma((4,)), dma((2,)), dma((2,)), dma((1,)), dma((2,)),
            dma((ITERS, 2)), dma((ITERS, 2)), dma((ITERS, 2)), dma((ITERS, 2)), dma((ITERS, 2)),
        ],
        compiler_params=pltpu.CompilerParams(collective_id=0, has_side_effects=True),
    )(held_tiles, placed, bin_mask.reshape(1, width), bias.reshape(1, width))

    left = strips - early_of(size)
    remain = jax.ShapeDtypeStruct((left, B, size), F32)

    def branch(k):
        sub, most = B // SUBS, max(k, 1)
        return lambda flags, pieces, held: pl.pallas_call(
            functools.partial(second, n, size, k),
            out_shape=(store, remain),
            in_specs=[smem, anywhere, anywhere],
            out_specs=(anywhere, anywhere),
            scratch_shapes=[
                pltpu.VMEM((strips, B, size), F32),
                pltpu.VMEM((most, B, size), F32),
                pltpu.VMEM((strips, B, size), F32),
                *[pltpu.VMEM((most, sub, size), F32) for _ in range(SUBS)],
                dma((1,)), dma((1 + SUBS,)), dma((2,)), dma((1,)), dma((2,)),
            ],
            compiler_params=pltpu.CompilerParams(collective_id=1 + k, has_side_effects=True, vmem_limit_bytes=GRANT),
        )(flags, pieces, held)

    whole = jax.ShapeDtypeStruct((rows_dev, 1, size, size), F32)

    def strip_scratch(slots):
        return [pltpu.VMEM((slots, B, size), F32), pltpu.VMEM((slots, B, size), F32), dma((slots,)), dma((slots,))]

    balanced = pl.pallas_call(
        functools.partial(third, size),
        out_shape=whole,
        in_specs=[vmem, vmem, vmem, anywhere],
        out_specs=anywhere,
        scratch_shapes=strip_scratch(strips),
    )(u, v, diag, arr0)
    flags, balanced = lax.optimization_barrier((flags, balanced))
    arr1, rest = lax.switch(flags[group], [branch(k) for k in range(group + 1)], flags, pieces, held_tiles)
    balanced, bias_new = pl.pallas_call(
        functools.partial(fourth, size),
        out_shape=(whole, wide),
        in_specs=[smem, vmem, vmem, vmem, vmem, anywhere, vmem, anywhere, anywhere],
        out_specs=(anywhere, vmem),
        scratch_shapes=strip_scratch(strips + left),
        input_output_aliases={8: 0},
        compiler_params=pltpu.CompilerParams(vmem_limit_bytes=GRANT),
    )(placed, u, v, diag, bias_new, arr1, rest, held_tiles, balanced)
    return balanced, bias_new.reshape(width)


def solution(mesh):
    specs = (P("bins", "diag", None, None), P("bins"), P("bins"), P("bins"))
    return jax.shard_map(
        functools.partial(local, mesh.shape["bins"]),
        mesh=mesh,
        in_specs=specs,
        out_specs=(P("bins", "diag", None, None), P("bins")),
        check_vma=False,
    )
```
